1024 devices in a mesh: lon: 32 (over y_lo, z, core), colat: 32 (over x, y_hi).
Axes of the slice: x: 8, y: 8 (y_hi: 4, y_lo: 2; y = y_hi * 2 + y_lo), z: 8, core: 2. Of those that a mesh axis runs over, the one named last changes fastest.
Arguments:
- forward_state: float32 [9, 8, 512, 4096], P(None, None, 'colat', 'lon'), may hold values from -6 to 6
- adjoint_state: float32 [9, 8, 512, 4096], P(None, None, 'colat', 'lon'), may hold values from -6 to 6
- layer_ids: int32 [8, 512, 4096], P(None, 'colat', 'lon'), may hold values from 0 to 15
- density_table: float32 [16], replicated, may hold values from 2 to 4
- lame_table: float32 [16], replicated, may hold values from 0.5 to 2
- shear_table: float32 [16], replicated, may hold values from 0.5 to 1.5
- source_cells: int32 [8], replicated, may hold values from 0 to 16777215
- source_wavelet: float32 [2, 8], replicated, may hold values from -6 to 6
- receiver_cells: int32 [512], replicated, may hold values from 0 to 16777215
- receiver_residual: float32 [2, 3, 512], replicated, may hold values from -6 to 6
Outputs:
- forward_field: float32 [9, 8, 512, 4096], P(None, None, 'colat', 'lon')
- adjoint_field: float32 [9, 8, 512, 4096], P(None, None, 'colat', 'lon')
- density_kernel: float32 [8, 512, 4096], P(None, 'colat', 'lon')
The draws below stay inside these ranges and needn't reach their ends.
Inputs may be any that keep to these rules, and one draw needn't show every extreme that they name: `source_cells`: flat index (level * 512 + colatitude) * 4096 + longitude. `receiver_cells`: flat index as for the sources.
All inputs are finite; a program needn't handle non-finite values.
Results may differ from the reference program's by a relative error of at most 0.0001.
Values sent between devices are 32-bit elements; how exact they have to be, the bound alone decides.
A program may use at most 32 MiB of HBM per device.

```python
import math
import jax
import jax.numpy as jnp

R = 8
STEPS = 2
NLAYER = 16
NSRC = 8
NREC = 512
NTH = 512
NPH = 4096


def place_ends(values, stream_key, low, high):
    dims = values.shape
    place = [jax.random.randint(jax.random.fold_in(stream_key, axis), (), 0, dims[axis]) for axis in range(len(dims))]
    values = values.at[tuple(place)].set(low)
    longest = dims.index(max(dims))
    place[longest] = (place[longest] + 1) % dims[longest]
    return values.at[tuple(place)].set(high)


def steps_of(own_key, dims, pieces, low, largest):
    factor_of, own = 1.0, jax.random.fold_in(own_key, 6)
    for dim, blocks in pieces:
        draws = jnp.exp(jax.random.uniform(jax.random.fold_in(own, dim), (blocks,), jnp.float32, low / len(pieces), largest / len(pieces)))
        factor_of = factor_of * jnp.repeat(draws, dims[dim] // blocks).reshape([-1 if axis == dim else 1 for axis in range(len(dims))])
    return factor_of


def scatter_about(key, dims, deviation, reach, cuts=(), kind=jnp.bfloat16):
    result = deviation * jax.random.normal(key, dims, jnp.float32)
    if cuts:
        result = result * steps_of(key, dims, cuts, -0.22, 0.18)
    return jnp.clip(result, -reach, reach).astype(kind)


def setup_inputs(seed: int = 0) -> dict:
    streams_of = jax.random.split(jax.random.key(seed), 11)
    forward_state = scatter_about(streams_of[0], (9, R, NTH, NPH), 1.0, 6.0, ((2, 32), (3, 32)), jnp.float32)
    adjoint_state = scatter_about(streams_of[1], (9, R, NTH, NPH), 1.0, 6.0, ((2, 32), (3, 32)), jnp.float32)
    layer_ids = place_ends(jax.random.randint(streams_of[2], (R, NTH, NPH), 0, NLAYER), jax.random.fold_in(streams_of[2], 1), 0, NLAYER - 1).astype(jnp.int32)
    density_table = jnp.clip(jax.random.uniform(streams_of[3], (NLAYER,), jnp.float32, 2.0, 4.0), 2.0, 4.0)
    lame_table = jnp.clip(jax.random.uniform(streams_of[4], (NLAYER,), jnp.float32, 0.5, 2.0), 0.5, 2.0)
    shear_table = jnp.clip(jax.random.uniform(streams_of[5], (NLAYER,), jnp.float32, 0.5, 1.5), 0.5, 1.5)
    source_cells = place_ends(jax.random.randint(streams_of[6], (NSRC,), 0, R * NTH * NPH), jax.random.fold_in(streams_of[6], 1), 0, (R * NTH * NPH) - 1).astype(jnp.int32)
    source_wavelet = scatter_about(streams_of[7], (STEPS, NSRC), 1.0, 6.0, (), jnp.float32)
    receiver_cells = place_ends(jax.random.randint(streams_of[8], (NREC,), 0, R * NTH * NPH), jax.random.fold_in(streams_of[8], 1), 0, (R * NTH * NPH) - 1).astype(jnp.int32)
    receiver_residual = scatter_about(streams_of[9], (STEPS, 3, NREC), 1.0, 6.0, (), jnp.float32)
    return dict(forward_state=forward_state, adjoint_state=adjoint_state, layer_ids=layer_ids, density_table=density_table, lame_table=lame_table, shear_table=shear_table, source_cells=source_cells, source_wavelet=source_wavelet, receiver_cells=receiver_cells, receiver_residual=receiver_residual)


R_INNER = 0.55
COURANT = 0.3
SIN_FLOOR = 0.25
VEL_SIGNS = (-1.0, -1.0, 1.0)
STRESS_SIGNS = (1.0, 1.0, 1.0, 1.0, -1.0, -1.0)


def geometry(row_ids, levels, lat_cells, lon_cells):
    theta_step = math.pi / lat_cells
    phi_step = 2.0 * math.pi / lon_cells
    delta_r = (1.0 - R_INNER) / levels
    radius = R_INNER + (jnp.arange(levels, dtype=jnp.float32) + 0.5) * delta_r
    colatitude = (row_ids.astype(jnp.float32) + 0.5) * theta_step
    sines_held = jnp.maximum(jnp.sin(colatitude), SIN_FLOOR)
    cotangent = jnp.cos(colatitude) / sines_held
    inv_radius = (1.0 / radius)[:, None, None]
    along_theta = inv_radius / theta_step
    along_phi = inv_radius / (sines_held[None, :, None] * phi_step)
    curvature = cotangent[None, :, None] * inv_radius
    return along_theta, along_phi, curvature, inv_radius, 1.0 / delta_r


def time_step(lon_cells):
    return COURANT * SIN_FLOOR * R_INNER * (2.0 * math.pi / lon_cells) / 1.6


def diff_theta(values):
    return (8.0 * (values[..., 3:-1, 2:-2] - values[..., 1:-3, 2:-2]) - (values[..., 4:, 2:-2] - values[..., :-4, 2:-2])) / 12.0


def diff_phi(values):
    return (8.0 * (values[..., 2:-2, 3:-1] - values[..., 2:-2, 1:-3]) - (values[..., 2:-2, 4:] - values[..., 2:-2, :-4])) / 12.0


def diff_radial(values):
    padded = jnp.pad(values, [(0, 0)] * (values.ndim - 3) + [(1, 1), (0, 0), (0, 0)])
    return (padded[..., 2:, :, :] - padded[..., :-2, :, :]) * 0.5


def accelerate(stress, metric):
    along_theta, along_phi, curvature, inv_radius, inv_spacing = metric
    centre_part = stress[..., 2:-2, 2:-2]
    stress_tt, stress_pp, stress_rr = centre_part[:, 0], centre_part[:, 1], centre_part[:, 2]
    stress_tp, stress_tr, stress_pr = centre_part[:, 3], centre_part[:, 4], centre_part[:, 5]
    theta_diff = diff_theta(stress)
    phi_diff = diff_phi(stress)
    radial_diff = diff_radial(centre_part)
    force_theta = along_theta * theta_diff[:, 0] + along_phi * phi_diff[:, 3] + inv_spacing * radial_diff[:, 4] + curvature * (stress_tt - stress_pp) + 3.0 * inv_radius * stress_tr
    force_phi = along_theta * theta_diff[:, 3] + along_phi * phi_diff[:, 1] + inv_spacing * radial_diff[:, 5] + 2.0 * curvature * stress_tp + 3.0 * inv_radius * stress_pr
    force_radial = along_theta * theta_diff[:, 4] + along_phi * phi_diff[:, 5] + inv_spacing * radial_diff[:, 2] + inv_radius * (2.0 * stress_rr - stress_tt - stress_pp) + curvature * stress_tr
    return jnp.stack([force_theta, force_phi, force_radial], 1)


def stress_rate(velocity, lame_field, shear_field, metric):
    along_theta, along_phi, curvature, inv_radius, inv_spacing = metric
    centre_part = velocity[..., 2:-2, 2:-2]
    vel_theta, vel_phi, vel_radial = centre_part[:, 0], centre_part[:, 1], centre_part[:, 2]
    theta_diff = diff_theta(velocity)
    phi_diff = diff_phi(velocity)
    radial_diff = diff_radial(centre_part)
    strain_tt = along_theta * theta_diff[:, 0] + inv_radius * vel_radial
    strain_pp = along_phi * phi_diff[:, 1] + curvature * vel_theta + inv_radius * vel_radial
    strain_rr = inv_spacing * radial_diff[:, 2]
    strain_tp = 0.5 * (along_theta * theta_diff[:, 1] - curvature * vel_phi + along_phi * phi_diff[:, 0])
    strain_tr = 0.5 * (inv_spacing * radial_diff[:, 0] - inv_radius * vel_theta + along_theta * theta_diff[:, 2])
    strain_pr = 0.5 * (inv_spacing * radial_diff[:, 1] - inv_radius * vel_phi + along_phi * phi_diff[:, 2])
    dilation = strain_tt + strain_pp + strain_rr
    double_shear = 2.0 * shear_field
    return jnp.stack([lame_field * dilation + double_shear * strain_tt, lame_field * dilation + double_shear * strain_pp,
                      lame_field * dilation + double_shear * strain_rr, double_shear * strain_tp,
                      double_shear * strain_tr, double_shear * strain_pr], 1)


def fold_rows(fields, rim_width, sign_flip):
    half_turn = fields.shape[-1] // 2
    upper_strip = jnp.roll(fields[..., :rim_width, :][..., ::-1, :], half_turn, axis=-1) * sign_flip
    lower_strip = jnp.roll(fields[..., -rim_width:, :][..., ::-1, :], half_turn, axis=-1) * sign_flip
    fields = jnp.concatenate([upper_strip, fields, lower_strip], -2)
    return jnp.concatenate([fields[..., -rim_width:], fields, fields[..., :rim_width]], -1)


def reference(forward_state, adjoint_state, layer_ids, density_table, lame_table, shear_table, source_cells, source_wavelet, receiver_cells, receiver_residual):
    levels, lat_cells, lon_cells = layer_ids.shape
    metric = geometry(jnp.arange(lat_cells, dtype=jnp.int32), levels, lat_cells, lon_cells)
    step_size = time_step(lon_cells)
    inv_rho = 1.0 / density_table[layer_ids]
    lame_field = lame_table[layer_ids]
    shear_field = shear_table[layer_ids]
    vel_flip = jnp.array(VEL_SIGNS, dtype=jnp.float32)[:, None, None, None]
    stress_flip = jnp.array(STRESS_SIGNS, dtype=jnp.float32)[:, None, None, None]
    stacked = jnp.stack([forward_state, adjoint_state])
    velocity = stacked[:, :3]
    stress = stacked[:, 3:]
    plane_cells = lat_cells * lon_cells
    source_level = source_cells // plane_cells
    source_row = (source_cells % plane_cells) // lon_cells
    source_col = source_cells % lon_cells
    receiver_level = receiver_cells // plane_cells
    receiver_row = (receiver_cells % plane_cells) // lon_cells
    receiver_col = receiver_cells % lon_cells
    kernel = jnp.zeros(layer_ids.shape, jnp.float32)
    for step_index in range(STEPS):
        forcing = accelerate(fold_rows(stress, 2, stress_flip), metric)
        velocity = velocity + step_size * inv_rho * forcing
        velocity = velocity.at[0, 2, source_level, source_row, source_col].add(source_wavelet[step_index])
        for component in range(3):
            velocity = velocity.at[1, component, receiver_level, receiver_row, receiver_col].add(receiver_residual[step_index, component])
        stress = stress + step_size * stress_rate(fold_rows(velocity, 2, vel_flip), lame_field, shear_field, metric)
        kernel = kernel + jnp.sum(velocity[0] * velocity[1], 0)
    forward_field = jnp.concatenate([velocity[0], stress[0]], 0)
    adjoint_field = jnp.concatenate([velocity[1], stress[1]], 0)
    return forward_field, adjoint_field, kernel
```

```python
import functools
import math

import jax
import jax.numpy as jnp
from jax import lax
from jax.experimental import pallas as pl
from jax.experimental.pallas import tpu as pltpu
from jax.sharding import PartitionSpec as P

STEPS = 2
R_INNER = 0.55
COURANT = 0.3
SIN_FLOOR = 0.25
MESH = pl.DeviceIdType.MESH
F32 = jnp.float32

LEV, ROWS, LANES = 8, 16, 128
TT, TR, TP, PP, PR, RR = range(6)
STATE_OF = (3, 7, 6, 4, 8, 5)
CHUNK = 4


def lane_roll(x, shift):
    return pltpu.roll(x, shift % LANES, x.ndim - 1)


def kernel(
    n_lon,
    n_lat,
    fwd_hbm,
    adj_hbm,
    ids_hbm,
    density_ref,
    lame_ref,
    shear_ref,
    src_ref,
    wave_ref,
    cells_ref,
    resid_ref,
    fwd_out,
    adj_out,
    kern_out,
    state_in,
    ids_in,
    state_o,
    kern_o,
    stress,
    vel,
    part_v,
    part_s,
    inject,
    source,
    coef,
    col_recv,
    lon_send,
    lon_recv,
    in_sem,
    out_sem,
    col_ssem,
    col_rsem,
    lon_ssem,
    lon_rsem,
):
    lon = lax.axis_index("lon")
    lat = lax.axis_index("colat")
    lat_cells, lon_cells = n_lat * ROWS, n_lon * LANES
    is_top = 1 - lax.div(lat + n_lat - 1, n_lat)
    is_bot = lax.div(lat + 1, n_lat)
    left = lax.rem(lon + n_lon - 1, n_lon)
    right = lax.rem(lon + 1, n_lon)
    up = {
        "lon": lax.rem(lon + is_top * (n_lon // 2), n_lon),
        "colat": lat - 1 + is_top,
    }
    down = {
        "lon": lax.rem(lon + is_bot * (n_lon // 2), n_lon),
        "colat": lat + 1 - is_bot,
    }
    to_left = {"lon": left, "colat": lat}
    to_right = {"lon": right, "colat": lat}

    barrier = pltpu.get_barrier_semaphore()
    for peer in (up, down, to_left, to_right):
        pl.semaphore_signal(barrier, inc=1, device_id=peer, device_id_type=MESH)

    loads = [
        pltpu.make_async_copy(fwd_hbm, state_in.at[0], in_sem.at[0]),
        pltpu.make_async_copy(adj_hbm, state_in.at[1], in_sem.at[1]),
        pltpu.make_async_copy(ids_hbm, ids_in, in_sem.at[2]),
    ]
    for load in loads:
        load.start()

    theta_step = math.pi / lat_cells
    phi_step = 2.0 * math.pi / lon_cells
    delta_r = (1.0 - R_INNER) / LEV
    step_size = COURANT * SIN_FLOOR * R_INNER * phi_step / 1.6
    level = lax.broadcasted_iota(jnp.int32, (LEV, LANES), 0)
    lane = lax.broadcasted_iota(jnp.int32, (LEV, LANES), 1)
    ir = 1.0 / (R_INNER + (level.astype(F32) + 0.5) * delta_r)
    at = ir * (1.0 / (12.0 * theta_step))
    c_up = jnp.where(level < LEV - 1, 0.5 / delta_r, 0.0).astype(F32)
    c_dn = jnp.where(level > 0, 0.5 / delta_r, 0.0).astype(F32)

    rows3 = lax.broadcasted_iota(jnp.int32, (ROWS, LEV, LANES), 0) + lat * ROWS
    theta = (rows3.astype(F32) + 0.5) * theta_step
    sines = jnp.maximum(jnp.sin(theta), SIN_FLOOR)
    coef[0] = ir[None] / (sines * (12.0 * phi_step))
    coef[1] = jnp.cos(theta) / sines * ir[None]

    for step in range(STEPS):
        for f in range(2):
            zero = jnp.zeros((3, 2, LEV, LANES), F32)
            stress[step, f, 0:3, 0:2] = zero
            stress[step, f, 0:3, ROWS + 2 : ROWS + 4] = zero
            vel[step, f, :, 0:2] = zero
            vel[step, f, :, ROWS + 2 : ROWS + 4] = zero

    def unpack_state(f):
        for c in range(6):
            for row in range(ROWS):
                start = STATE_OF[c] * (LEV * ROWS) + row
                stress[0, f, c, 2 + row] = state_in[f, pl.ds(start, LEV, stride=ROWS), :]

    def send_cols(phase, f, ref):
        dst_slot = 1 - is_top
        a = pltpu.make_async_remote_copy(
            src_ref=ref.at[0:3, 2:4],
            dst_ref=col_recv.at[phase, f, dst_slot],
            send_sem=col_ssem.at[phase, f, 0],
            recv_sem=col_rsem.at[phase, f, dst_slot],
            device_id=up,
            device_id_type=MESH,
        )
        b = pltpu.make_async_remote_copy(
            src_ref=ref.at[0:3, ROWS : ROWS + 2],
            dst_ref=col_recv.at[phase, f, is_bot],
            send_sem=col_ssem.at[phase, f, 1],
            recv_sem=col_rsem.at[phase, f, is_bot],
            device_id=down,
            device_id_type=MESH,
        )
        a.start()
        b.start()
        return [a, b]

    quad = lax.div(lane, 4)
    spot = lax.rem(lane, 4)

    def pack_rim(rows_of):
        packed = []
        for group in range(2):
            acc = jnp.zeros((LEV, LANES), F32)
            for slot in range(32):
                k = group * 32 + slot
                if k < 48:
                    acc = jnp.where(quad == slot, lane_roll(rows_of(k // ROWS, k % ROWS), 4 * slot + 2), acc)
            packed.append(acc)
        return packed

    def send_lons(phase, f, rows_of):
        packed = pack_rim(rows_of)
        for group in range(2):
            lon_send[phase, f, group] = packed[group]
        copies = []
        for slot, peer in ((0, to_right), (1, to_left)):
            copy = pltpu.make_async_remote_copy(
                src_ref=lon_send.at[phase, f],
                dst_ref=lon_recv.at[phase, f, slot],
                send_sem=lon_ssem.at[phase, f, slot],
                recv_sem=lon_rsem.at[phase, f, slot],
                device_id=peer,
                device_id_type=MESH,
            )
            copy.start()
            copies.append(copy)
        return copies

    def wait_halo(phase, f):
        for slot in range(2):
            pltpu.make_async_remote_copy(
                src_ref=col_recv.at[phase, f, slot],
                dst_ref=col_recv.at[phase, f, slot],
                send_sem=col_ssem.at[phase, f, slot],
                recv_sem=col_rsem.at[phase, f, slot],
                device_id=up,
                device_id_type=MESH,
            ).wait_recv()
            pltpu.make_async_remote_copy(
                src_ref=lon_send.at[phase, f],
                dst_ref=lon_recv.at[phase, f, slot],
                send_sem=lon_ssem.at[phase, f, slot],
                recv_sem=lon_rsem.at[phase, f, slot],
                device_id=to_left,
                device_id_type=MESH,
            ).wait_recv()

    def rim_terms(phase, f):
        out = []
        for group in range(2):
            own = lon_send[phase, f, group]
            halo = jnp.where(spot < 2, lon_recv[phase, f, 0, group], lon_recv[phase, f, 1, group]) - own
            next1, next2 = lane_roll(halo, -1), lane_roll(halo, -2)
            prev1, prev2 = lane_roll(halo, 1), lane_roll(halo, 2)
            term = jnp.where(
                spot == 0,
                -next2,
                jnp.where(spot == 1, 8.0 * next1 - next2, jnp.where(spot == 2, prev2 - 8.0 * prev1, prev2)),
            )
            out.append(term)
        return out

    edge = (lane < 2) | (lane >= LANES - 2)

    def rim_of(terms, c, row):
        k = c * ROWS + row
        return jnp.where(edge, lane_roll(terms[k // 32], -(4 * (k % 32) + 2)), 0.0)

    def band_terms(phase, f, signs):
        flip_top = 1.0 - 2.0 * is_top.astype(F32)
        flip_bot = 1.0 - 2.0 * is_bot.astype(F32)
        terms = {}
        for c in range(3):
            near_top = col_recv[phase, f, 0, c, 1 - is_top]
            far_top = col_recv[phase, f, 0, c, is_top]
            near_bot = col_recv[phase, f, 1, c, is_bot]
            far_bot = col_recv[phase, f, 1, c, 1 - is_bot]
            if signs[c] < 0:
                near_top, far_top = near_top * flip_top, far_top * flip_top
                near_bot, far_bot = near_bot * flip_bot, far_bot * flip_bot
            terms[c, 0] = far_top - 8.0 * near_top
            terms[c, 1] = near_top
            terms[c, ROWS - 2] = -near_bot
            terms[c, ROWS - 1] = 8.0 * near_bot - far_bot
        return terms

    def diff_t(ref, c, r0, n):
        return 8.0 * (ref[c, pl.ds(r0 + 3, n)] - ref[c, pl.ds(r0 + 1, n)]) - (
            ref[c, pl.ds(r0 + 4, n)] - ref[c, pl.ds(r0, n)]
        )

    def diff_p(x):
        return 8.0 * (lane_roll(x, -1) - lane_roll(x, 1)) - (lane_roll(x, -2) - lane_roll(x, 2))

    def diff_r(x):
        return c_up * pltpu.roll(x, LEV - 1, 1) - c_dn * pltpu.roll(x, 1, 1)

    def local_velocity(step, f):
        ref = stress.at[step, f]

        def body(i, carry):
            r0 = i * CHUNK
            own = pl.ds(r0, CHUNK)
            ap, cv = coef[0, own], coef[1, own]
            tt, tr, tp, pp, pr, rr = (ref[c, pl.ds(r0 + 2, CHUNK)] for c in range(6))
            f_t = at * diff_t(ref, TT, r0, CHUNK) + ap * diff_p(tp) + diff_r(tr) + cv * (tt - pp) + (3.0 * ir) * tr
            f_p = at * diff_t(ref, TP, r0, CHUNK) + ap * diff_p(pp) + diff_r(pr) + 2.0 * cv * tp + (3.0 * ir) * pr
            f_r = (
                at * diff_t(ref, TR, r0, CHUNK)
                + ap * diff_p(pr)
                + diff_r(rr)
                + ir * (2.0 * rr - tt - pp)
                + cv * tr
            )
            scale = coef[2, own]
            for c, force in enumerate((f_t, f_p, f_r)):
                value = scale * force
                if step > 0:
                    value = value + vel[step - 1, f, c, pl.ds(r0 + 2, CHUNK)]
                if f == 0:
                    if c == 2:
                        value = value + source[step, own]
                else:
                    value = value + inject[step, c, own]
                part_v[f, c, own] = value
            return carry

        lax.fori_loop(0, ROWS // CHUNK, body, 0)

        if step == 0:
            for c in range(3):
                for row in range(ROWS):
                    part_v[f, c, row] += state_in[f, pl.ds(c * (LEV * ROWS) + row, LEV, stride=ROWS), :]

    BOUNDARY = (0, 1, ROWS - 2, ROWS - 1)
    INNER = tuple(range(2, ROWS - 2))

    def finish_velocity(step, f):
        phase = 2 * step
        rims = rim_terms(phase, f)
        bands = band_terms(phase, f, (1, -1, 1))
        band_of = (TT, TP, TR)
        rim_index = (0, 1, 2)
        copies = []
        for rows in (BOUNDARY, INNER):
            for row in rows:
                for c in range(3):
                    extra = coef[0, row] * rim_of(rims, rim_index[c], row)
                    if rows is BOUNDARY:
                        extra = extra + at * bands[band_of[c], row]
                    vel[step, f, c, 2 + row] = part_v[f, c, row] + coef[2, row] * extra
            if rows is BOUNDARY:
                copies += send_cols(phase + 1, f, vel.at[step, f])
        copies += send_lons(phase + 1, f, lambda c, row: vel[step, f, c, 2 + row])
        return copies

    def local_stress(step, f):
        ref = vel.at[step, f]
        old = stress.at[step, f]

        def body(i, carry):
            r0 = i * CHUNK
            own = pl.ds(r0, CHUNK)
            mid = pl.ds(r0 + 2, CHUNK)
            ap, cv = coef[0, own], coef[1, own]
            lam, mu2 = coef[3, own], coef[4, own]
            vt, vp, vr = (ref[c, mid] for c in range(3))
            e_tt = at * diff_t(ref, 0, r0, CHUNK) + ir * vr
            e_pp = ap * diff_p(vp) + cv * vt + ir * vr
            e_rr = diff_r(vr)
            e_tp = at * diff_t(ref, 1, r0, CHUNK) - cv * vp + ap * diff_p(vt)
            e_tr = diff_r(vt) - ir * vt + at * diff_t(ref, 2, r0, CHUNK)
            e_pr = diff_r(vp) - ir * vp + ap * diff_p(vr)
            dil = lam * (e_tt + e_pp + e_rr)
            half = 0.5 * mu2
            part_s[f, TT, own] = old[TT, mid] + (dil + mu2 * e_tt)
            part_s[f, PP, own] = old[PP, mid] + (dil + mu2 * e_pp)
            part_s[f, RR, own] = old[RR, mid] + (dil + mu2 * e_rr)
            part_s[f, TP, own] = old[TP, mid] + half * e_tp
            part_s[f, TR, own] = old[TR, mid] + half * e_tr
            part_s[f, PR, own] = old[PR, mid] + half * e_pr
            return carry

        lax.fori_loop(0, ROWS // CHUNK, body, 0)

    def finish_stress(step, f):
        phase = 2 * step + 1
        last = step == STEPS - 1
        rims = rim_terms(phase, f)
        bands = band_terms(phase, f, (-1, -1, 1))
        copies = []

        def put(c, row, value):
            if last:
                state_o[f, pl.ds(STATE_OF[c] * (LEV * ROWS) + row, LEV, stride=ROWS), :] = value
            else:
                stress[step + 1, f, c, 2 + row] = value

        for rows in (BOUNDARY, INNER):
            for row in rows:
                ap, lam, mu2 = coef[0, row], coef[3, row], coef[4, row]
                half = 0.5 * mu2
                d_p = [ap * rim_of(rims, c, row) for c in range(3)]
                if rows is BOUNDARY:
                    d_t = [at * bands[c, row] for c in range(3)]
                    dil = lam * (d_t[0] + d_p[1])
                    put(TT, row, part_s[f, TT, row] + (dil + mu2 * d_t[0]))
                    put(TP, row, part_s[f, TP, row] + half * (d_t[1] + d_p[0]))
                    put(TR, row, part_s[f, TR, row] + half * d_t[2])
                else:
                    dil = lam * d_p[1]
                    put(TT, row, part_s[f, TT, row] + dil)
                    put(TP, row, part_s[f, TP, row] + half * d_p[0])
                    put(TR, row, part_s[f, TR, row])
                put(PP, row, part_s[f, PP, row] + (dil + mu2 * d_p[1]))
                put(RR, row, part_s[f, RR, row] + dil)
                put(PR, row, part_s[f, PR, row] + half * d_p[2])
            if rows is BOUNDARY and not last:
                copies += send_cols(phase + 1, f, stress.at[step + 1, f])
        if not last:
            copies += send_lons(phase + 1, f, lambda c, row: stress[step + 1, f, TP + c, 2 + row])
        return copies

    def materials():
        def body(row, carry):
            ids = ids_in[pl.ds(row, LEV, stride=ROWS), :]
            rho = jnp.zeros((LEV, LANES), F32)
            lam, mu = rho, rho
            for layer in range(16):
                hit = ids == layer
                rho = jnp.where(hit, density_ref[layer], rho)
                lam = jnp.where(hit, lame_ref[layer], lam)
                mu = jnp.where(hit, shear_ref[layer], mu)
            coef[2, row] = step_size * (1.0 / rho)
            coef[3, row] = step_size * lam
            coef[4, row] = (2.0 * step_size) * mu
            return carry

        lax.fori_loop(0, ROWS, body, 0)

    def injection():
        plane = lat_cells * lon_cells
        rows = lax.broadcasted_iota(jnp.int32, (ROWS, LEV, LANES), 0) + lat * ROWS
        levels = lax.broadcasted_iota(jnp.int32, (ROWS, LEV, LANES), 1)
        lanes = lax.broadcasted_iota(jnp.int32, (ROWS, LEV, LANES), 2) + lon * LANES
        cell = levels * plane + rows * lon_cells + lanes
        adds = [jnp.zeros((ROWS, LEV, LANES), F32) for _ in range(STEPS)]
        for s in range(src_ref.shape[0]):
            hit = cell == src_ref[s]
            for step in range(STEPS):
                adds[step] = adds[step] + jnp.where(hit, wave_ref[step, s], 0.0)
        for step in range(STEPS):
            source[step] = adds[step]
        cells = cells_ref[...].reshape(1, -1)
        count = cells.shape[1]
        lev_n = lax.div(cells, plane)
        in_plane = cells - lev_n * plane
        row_n = lax.div(in_plane, lon_cells)
        col_n = in_plane - row_n * lon_cells - lon * LANES
        row_n = row_n - lat * ROWS
        inside = (row_n >= 0) & (row_n < ROWS)
        place_n = jnp.where(inside, row_n * LEV + lev_n, -1)
        index = lax.broadcasted_iota(jnp.int32, (LANES, count), 0)
        lane_hot = jnp.where(index == col_n, 1.0, 0.0).astype(jnp.bfloat16)
        place_hit = index == place_n
        for step in range(STEPS):
            for c in range(3):
                values = resid_ref[c, pl.ds(step, 1)]
                high = values.astype(jnp.bfloat16).astype(F32)
                rest = values - high
                middle = rest.astype(jnp.bfloat16).astype(F32)
                total = None
                for term in (high, middle, rest - middle):
                    left_hot = jnp.where(place_hit, term, 0.0).astype(jnp.bfloat16)
                    piece = lax.dot_general(
                        left_hot, lane_hot, (((1,), (1,)), ((), ())), preferred_element_type=F32
                    )
                    total = piece if total is None else total + piece
                inject[step, c] = total.reshape(ROWS, LEV, LANES)

    started = []
    loads[0].wait()
    unpack_state(0)
    loads[1].wait()
    unpack_state(1)
    pl.semaphore_wait(barrier, 4)
    for f in range(2):
        started += send_cols(0, f, stress.at[0, f])
        started += send_lons(0, f, lambda c, row: stress[0, f, TP + c, 2 + row])
    loads[2].wait()
    materials()
    injection()
    outs = []
    for step in range(STEPS):
        for f in range(2):
            local_velocity(step, f)
        for f in range(2):
            wait_halo(2 * step, f)
            started += finish_velocity(step, f)
            local_stress(step, f)
        if step == STEPS - 1:
            for row in range(ROWS):
                density = None
                for s in range(STEPS):
                    for c in range(3):
                        term = vel[s, 0, c, 2 + row] * vel[s, 1, c, 2 + row]
                        density = term if density is None else density + term
                kern_o[pl.ds(row, LEV, stride=ROWS), :] = density
                for f in range(2):
                    for c in range(3):
                        state_o[f, pl.ds(c * (LEV * ROWS) + row, LEV, stride=ROWS), :] = vel[step, f, c, 2 + row]
            velocity_rows = pl.ds(0, 3 * LEV * ROWS)
            stress_rows = pl.ds(3 * LEV * ROWS, 6 * LEV * ROWS)
            outs.append(pltpu.make_async_copy(kern_o, kern_out, out_sem.at[0]))
            for f, out in enumerate((fwd_out, adj_out)):
                outs.append(
                    pltpu.make_async_copy(state_o.at[f, velocity_rows], out.at[velocity_rows], out_sem.at[1 + f])
                )
            for copy in outs:
                copy.start()
        for f in range(2):
            wait_halo(2 * step + 1, f)
            started += finish_stress(step, f)
            if step == STEPS - 1:
                out = (fwd_out, adj_out)[f]
                copy = pltpu.make_async_copy(state_o.at[f, stress_rows], out.at[stress_rows], out_sem.at[3 + f])
                copy.start()
                outs.append(copy)
    for copy in started:
        copy.wait_send()
    for copy in outs:
        copy.wait()


def on_device(n_lon, n_lat, forward, adjoint, layer_ids, density, lame, shear, src, wave, cells, resid):
    flat = 9 * LEV * ROWS
    vmem = pl.BlockSpec(memory_space=pltpu.VMEM)
    smem = pl.BlockSpec(memory_space=pltpu.SMEM)
    hbm = pl.BlockSpec(memory_space=pl.ANY)
    phases = 2 * STEPS
    fwd, adj, kern = pl.pallas_call(
        functools.partial(kernel, n_lon, n_lat),
        out_shape=(
            jax.ShapeDtypeStruct((flat, LANES), F32),
            jax.ShapeDtypeStruct((flat, LANES), F32),
            jax.ShapeDtypeStruct((LEV * ROWS, LANES), F32),
        ),
        in_specs=[hbm, hbm, hbm, smem, smem, smem, smem, smem, vmem, vmem],
        out_specs=(hbm, hbm, hbm),
        scratch_shapes=[
            pltpu.VMEM((2, flat, LANES), F32),
            pltpu.VMEM((LEV * ROWS, LANES), jnp.int32),
            pltpu.VMEM((2, flat, LANES), F32),
            pltpu.VMEM((LEV * ROWS, LANES), F32),
            pltpu.VMEM((STEPS, 2, 6, ROWS + 4, LEV, LANES), F32),
            pltpu.VMEM((STEPS, 2, 3, ROWS + 4, LEV, LANES), F32),
            pltpu.VMEM((2, 3, ROWS, LEV, LANES), F32),
            pltpu.VMEM((2, 6, ROWS, LEV, LANES), F32),
            pltpu.VMEM((STEPS, 3, ROWS, LEV, LANES), F32),
            pltpu.VMEM((STEPS, ROWS, LEV, LANES), F32),
            pltpu.VMEM((5, ROWS, LEV, LANES), F32),
            pltpu.VMEM((phases, 2, 2, 3, 2, LEV, LANES), F32),
            pltpu.VMEM((phases, 2, 2, LEV, LANES), F32),
            pltpu.VMEM((phases, 2, 2, 2, LEV, LANES), F32),
            pltpu.SemaphoreType.DMA((3,)),
            pltpu.SemaphoreType.DMA((5,)),
            pltpu.SemaphoreType.DMA((phases, 2, 2)),
            pltpu.SemaphoreType.DMA((phases, 2, 2)),
            pltpu.SemaphoreType.DMA((phases, 2, 2)),
            pltpu.SemaphoreType.DMA((phases, 2, 2)),
        ],
        compiler_params=pltpu.CompilerParams(collective_id=0, has_side_effects=True),
        name="elastic_steps",
    )(
        forward.reshape(flat, LANES),
        adjoint.reshape(flat, LANES),
        layer_ids.reshape(LEV * ROWS, LANES),
        density,
        lame,
        shear,
        src,
        wave,
        cells,
        jnp.transpose(resid, (1, 0, 2)),
    )
    return fwd.reshape(forward.shape), adj.reshape(adjoint.shape), kern.reshape(layer_ids.shape)


def solution(mesh):
    field = P(None, None, "colat", "lon")
    plane = P(None, "colat", "lon")
    return jax.shard_map(
        functools.partial(on_device, mesh.shape["lon"], mesh.shape["colat"]),
        mesh=mesh,
        in_specs=(field, field, plane) + (P(),) * 7,
        out_specs=(field, field, plane),
        check_vma=False,
    )
```

```python
import functools
import math

import jax
import jax.numpy as jnp
from jax import lax
from jax.experimental import pallas as pl
from jax.experimental.pallas import tpu as pltpu
from jax.sharding import PartitionSpec as P

STEPS = 2
R_INNER = 0.55
COURANT = 0.3
SIN_FLOOR = 0.25
MESH = pl.DeviceIdType.MESH
F32 = jnp.float32

LEV, ROWS, LANES = 8, 16, 128
TT, TR, TP, PP, PR, RR = range(6)
STATE_OF = (3, 7, 6, 4, 8, 5)
CHUNK = 4


def lane_roll(x, shift):
    return pltpu.roll(x, shift % LANES, x.ndim - 1)


def kernel(
    n_lon,
    n_lat,
    fwd_hbm,
    adj_hbm,
    ids_hbm,
    density_ref,
    lame_ref,
    shear_ref,
    src_ref,
    wave_ref,
    cells_ref,
    resid_ref,
    state_o,
    kern_o,
    state_in,
    ids_in,
    stress,
    vel,
    part_v,
    part_s,
    inject,
    source,
    coef,
    part_rim,
    coef_rim,
    col_recv,
    lon_send,
    lon_recv,
    in_sem,
    col_ssem,
    col_rsem,
    lon_ssem,
    lon_rsem,
):
    lon = lax.axis_index("lon")
    lat = lax.axis_index("colat")
    lat_cells, lon_cells = n_lat * ROWS, n_lon * LANES
    is_top = 1 - lax.div(lat + n_lat - 1, n_lat)
    is_bot = lax.div(lat + 1, n_lat)
    left = lax.rem(lon + n_lon - 1, n_lon)
    right = lax.rem(lon + 1, n_lon)
    up = {
        "lon": lax.rem(lon + is_top * (n_lon // 2), n_lon),
        "colat": lat - 1 + is_top,
    }
    down = {
        "lon": lax.rem(lon + is_bot * (n_lon // 2), n_lon),
        "colat": lat + 1 - is_bot,
    }
    to_left = {"lon": left, "colat": lat}
    to_right = {"lon": right, "colat": lat}

    barrier = pltpu.get_barrier_semaphore()
    for peer in (up, down, to_left, to_right):
        pl.semaphore_signal(barrier, inc=1, device_id=peer, device_id_type=MESH)

    velocity_rows = pl.ds(0, 3 * LEV * ROWS)
    stress_rows = pl.ds(3 * LEV * ROWS, 6 * LEV * ROWS)
    loads = [
        pltpu.make_async_copy(fwd_hbm.at[stress_rows], state_in.at[0, stress_rows], in_sem.at[0]),
        pltpu.make_async_copy(adj_hbm.at[stress_rows], state_in.at[1, stress_rows], in_sem.at[1]),
        pltpu.make_async_copy(ids_hbm, ids_in, in_sem.at[2]),
        pltpu.make_async_copy(fwd_hbm.at[velocity_rows], state_in.at[0, velocity_rows], in_sem.at[3]),
        pltpu.make_async_copy(adj_hbm.at[velocity_rows], state_in.at[1, velocity_rows], in_sem.at[4]),
    ]
    for load in loads:
        load.start()

    theta_step = math.pi / lat_cells
    phi_step = 2.0 * math.pi / lon_cells
    delta_r = (1.0 - R_INNER) / LEV
    step_size = COURANT * SIN_FLOOR * R_INNER * phi_step / 1.6
    level = lax.broadcasted_iota(jnp.int32, (LEV, LANES), 0)
    lane = lax.broadcasted_iota(jnp.int32, (LEV, LANES), 1)
    ir = 1.0 / (R_INNER + (level.astype(F32) + 0.5) * delta_r)
    at = ir * (1.0 / (12.0 * theta_step))
    c_up = jnp.where(level < LEV - 1, 0.5 / delta_r, 0.0).astype(F32)
    c_dn = jnp.where(level > 0, 0.5 / delta_r, 0.0).astype(F32)

    rows3 = lax.broadcasted_iota(jnp.int32, (ROWS, LEV, LANES), 0) + lat * ROWS
    theta = (rows3.astype(F32) + 0.5) * theta_step
    sines = jnp.maximum(jnp.sin(theta), SIN_FLOOR)
    coef[0] = ir[None] / (sines * (12.0 * phi_step))
    coef[1] = jnp.cos(theta) / sines * ir[None]

    for step in range(STEPS):
        for f in range(2):
            zero = jnp.zeros((3, 2, LEV, LANES), F32)
            stress[step, f, 0:3, 0:2] = zero
            stress[step, f, 0:3, ROWS + 2 : ROWS + 4] = zero
            vel[step, f, :, 0:2] = zero
            vel[step, f, :, ROWS + 2 : ROWS + 4] = zero

    BOUNDARY = (0, 1, ROWS - 2, ROWS - 1)
    INNER = tuple(range(2, ROWS - 2))

    def unpack_stress(f, comps, rows):
        for c in comps:
            for row in rows:
                start = STATE_OF[c] * (LEV * ROWS) + row
                stress[0, f, c, 2 + row] = state_in[f, pl.ds(start, LEV, stride=ROWS), :]

    def send_cols(phase, f, ref):
        dst_slot = 1 - is_top
        a = pltpu.make_async_remote_copy(
            src_ref=ref.at[0:3, 2:4],
            dst_ref=col_recv.at[phase, f, dst_slot],
            send_sem=col_ssem.at[phase, f, 0],
            recv_sem=col_rsem.at[phase, f, dst_slot],
            device_id=up,
            device_id_type=MESH,
        )
        b = pltpu.make_async_remote_copy(
            src_ref=ref.at[0:3, ROWS : ROWS + 2],
            dst_ref=col_recv.at[phase, f, is_bot],
            send_sem=col_ssem.at[phase, f, 1],
            recv_sem=col_rsem.at[phase, f, is_bot],
            device_id=down,
            device_id_type=MESH,
        )
        a.start()
        b.start()
        return [a, b]

    quad = lax.div(lane, 4)
    spot = lax.rem(lane, 4)

    def pack_rim(base, rows, row_of):
        packed = []
        for group in range(2):
            acc = base[group]
            for slot in range(32):
                c, row = divmod(group * 32 + slot, ROWS)
                if c < 3 and row in rows:
                    acc = jnp.where(quad == slot, lane_roll(row_of(c, row), 4 * slot + 2), acc)
            packed.append(acc)
        return packed

    blank = [jnp.zeros((LEV, LANES), F32)] * 2

    def send_lons(phase, f):
        copies = []
        for slot, peer in ((0, to_right), (1, to_left)):
            copy = pltpu.make_async_remote_copy(
                src_ref=lon_send.at[phase, f],
                dst_ref=lon_recv.at[phase, f, slot],
                send_sem=lon_ssem.at[phase, f, slot],
                recv_sem=lon_rsem.at[phase, f, slot],
                device_id=peer,
                device_id_type=MESH,
            )
            copy.start()
            copies.append(copy)
        return copies

    def wait_halo(phase, f):
        for slot in range(2):
            pltpu.make_async_remote_copy(
                src_ref=col_recv.at[phase, f, slot],
                dst_ref=col_recv.at[phase, f, slot],
                send_sem=col_ssem.at[phase, f, slot],
                recv_sem=col_rsem.at[phase, f, slot],
                device_id=up,
                device_id_type=MESH,
            ).wait_recv()
            pltpu.make_async_remote_copy(
                src_ref=lon_send.at[phase, f],
                dst_ref=lon_recv.at[phase, f, slot],
                send_sem=lon_ssem.at[phase, f, slot],
                recv_sem=lon_rsem.at[phase, f, slot],
                device_id=to_left,
                device_id_type=MESH,
            ).wait_recv()

    def rim_terms(phase, f):
        out = []
        for group in range(2):
            own = lon_send[phase, f, group]
            halo = jnp.where(spot < 2, lon_recv[phase, f, 0, group], lon_recv[phase, f, 1, group]) - own
            next1, next2 = lane_roll(halo, -1), lane_roll(halo, -2)
            prev1, prev2 = lane_roll(halo, 1), lane_roll(halo, 2)
            term = jnp.where(
                spot == 0,
                -next2,
                jnp.where(spot == 1, 8.0 * next1 - next2, jnp.where(spot == 2, prev2 - 8.0 * prev1, prev2)),
            )
            out.append(term)
        return out

    edge = (lane < 2) | (lane >= LANES - 2)

    def rim_of(terms, c, row):
        k = c * ROWS + row
        return jnp.where(edge, lane_roll(terms[k // 32], -(4 * (k % 32) + 2)), 0.0)

    def band_terms(phase, f, signs):
        flip_top = 1.0 - 2.0 * is_top.astype(F32)
        flip_bot = 1.0 - 2.0 * is_bot.astype(F32)
        terms = {}
        for c in range(3):
            near_top = col_recv[phase, f, 0, c, 1 - is_top]
            far_top = col_recv[phase, f, 0, c, is_top]
            near_bot = col_recv[phase, f, 1, c, is_bot]
            far_bot = col_recv[phase, f, 1, c, 1 - is_bot]
            if signs[c] < 0:
                near_top, far_top = near_top * flip_top, far_top * flip_top
                near_bot, far_bot = near_bot * flip_bot, far_bot * flip_bot
            terms[c, 0] = far_top - 8.0 * near_top
            terms[c, 1] = near_top
            terms[c, ROWS - 2] = -near_bot
            terms[c, ROWS - 1] = 8.0 * near_bot - far_bot
        return terms

    def diff_t(ref, c, r0, n):
        return 8.0 * (ref[c, pl.ds(r0 + 3, n)] - ref[c, pl.ds(r0 + 1, n)]) - (
            ref[c, pl.ds(r0 + 4, n)] - ref[c, pl.ds(r0, n)]
        )

    def diff_p(x):
        return 8.0 * (lane_roll(x, -1) - lane_roll(x, 1)) - (lane_roll(x, -2) - lane_roll(x, 2))

    def diff_r(x):
        return c_up * pltpu.roll(x, LEV - 1, 1) - c_dn * pltpu.roll(x, 1, 1)

    def local_velocity(step, f):
        ref = stress.at[step, f]

        def body(i, carry):
            r0 = i * CHUNK
            own = pl.ds(r0, CHUNK)
            ap, cv = coef[0, own], coef[1, own]
            tt, tr, tp, pp, pr, rr = (ref[c, pl.ds(r0 + 2, CHUNK)] for c in range(6))
            f_t = at * diff_t(ref, TT, r0, CHUNK) + ap * diff_p(tp) + diff_r(tr) + cv * (tt - pp) + (3.0 * ir) * tr
            f_p = at * diff_t(ref, TP, r0, CHUNK) + ap * diff_p(pp) + diff_r(pr) + 2.0 * cv * tp + (3.0 * ir) * pr
            f_r = (
                at * diff_t(ref, TR, r0, CHUNK)
                + ap * diff_p(pr)
                + diff_r(rr)
                + ir * (2.0 * rr - tt - pp)
                + cv * tr
            )
            scale = coef[2, own]
            for c, force in enumerate((f_t, f_p, f_r)):
                value = scale * force
                if step > 0:
                    value = value + vel[step - 1, f, c, pl.ds(r0 + 2, CHUNK)]
                if f == 0:
                    if c == 2:
                        value = value + source[step, own]
                else:
                    value = value + inject[step, c, own]
                part_v[f, c, own] = value
            return carry

        lax.fori_loop(0, ROWS // CHUNK, body, 0)

        if step == 0:
            for c in range(3):
                for row in range(ROWS):
                    part_v[f, c, row] += state_in[f, pl.ds(c * (LEV * ROWS) + row, LEV, stride=ROWS), :]
        packed = pack_rim(blank, INNER, lambda c, row: part_v[f, c, row])
        for group in range(2):
            part_rim[f, group] = packed[group]

    def send_finished(phase, f, kind, rims, ref, lon_row):
        base = [part_rim[f, group] + coef_rim[kind, group] * rims[group] for group in range(2)]
        packed = pack_rim(base, BOUNDARY, lon_row)
        for group in range(2):
            lon_send[phase + 1, f, group] = packed[group]
        return send_cols(phase + 1, f, ref) + send_lons(phase + 1, f)

    def finish_velocity(step, f, rows, rims, bands=None):
        band_of = (TT, TP, TR)
        done = {}
        for row in rows:
            for c in range(3):
                extra = coef[0, row] * rim_of(rims, c, row)
                if bands is not None:
                    extra = extra + at * bands[band_of[c], row]
                done[c, row] = part_v[f, c, row] + coef[2, row] * extra
                vel[step, f, c, 2 + row] = done[c, row]
        return done

    def edges_velocity(step, f):
        phase = 2 * step
        wait_halo(phase, f)
        rims = rim_terms(phase, f)
        done = finish_velocity(step, f, BOUNDARY, rims, band_terms(phase, f, (1, -1, 1)))
        copies = send_finished(phase, f, 0, rims, vel.at[step, f], lambda c, row: done[c, row])
        return rims, copies

    def local_stress(step, f):
        ref = vel.at[step, f]
        old = stress.at[step, f]

        def body(i, carry):
            r0 = i * CHUNK
            own = pl.ds(r0, CHUNK)
            mid = pl.ds(r0 + 2, CHUNK)
            ap, cv = coef[0, own], coef[1, own]
            lam, mu2 = coef[3, own], coef[4, own]
            vt, vp, vr = (ref[c, mid] for c in range(3))
            e_tt = at * diff_t(ref, 0, r0, CHUNK) + ir * vr
            e_pp = ap * diff_p(vp) + cv * vt + ir * vr
            e_rr = diff_r(vr)
            e_tp = at * diff_t(ref, 1, r0, CHUNK) - cv * vp + ap * diff_p(vt)
            e_tr = diff_r(vt) - ir * vt + at * diff_t(ref, 2, r0, CHUNK)
            e_pr = diff_r(vp) - ir * vp + ap * diff_p(vr)
            dil = lam * (e_tt + e_pp + e_rr)
            half = 0.5 * mu2
            part_s[f, TT, own] = old[TT, mid] + (dil + mu2 * e_tt)
            part_s[f, PP, own] = old[PP, mid] + (dil + mu2 * e_pp)
            part_s[f, RR, own] = old[RR, mid] + (dil + mu2 * e_rr)
            part_s[f, TP, own] = old[TP, mid] + half * e_tp
            part_s[f, TR, own] = old[TR, mid] + half * e_tr
            part_s[f, PR, own] = old[PR, mid] + half * e_pr
            return carry

        lax.fori_loop(0, ROWS // CHUNK, body, 0)
        if step < STEPS - 1:
            packed = pack_rim(blank, INNER, lambda c, row: part_s[f, TP + c, row])
            for group in range(2):
                part_rim[f, group] = packed[group]
        else:
            for row in INNER:
                start = STATE_OF[TR] * (LEV * ROWS) + row
                state_o[f, pl.ds(start, LEV, stride=ROWS), :] = part_s[f, TR, row]

    def finish_stress(step, f, rows, rims, bands=None):
        last = step == STEPS - 1
        done = {}

        def put(c, row, value):
            done[c, row] = value
            if last:
                state_o[f, pl.ds(STATE_OF[c] * (LEV * ROWS) + row, LEV, stride=ROWS), :] = value
            else:
                stress[step + 1, f, c, 2 + row] = value

        for row in rows:
            ap, lam, mu2 = coef[0, row], coef[3, row], coef[4, row]
            half = 0.5 * mu2
            d_p = [ap * rim_of(rims, c, row) for c in range(3)]
            if bands is not None:
                d_t = [at * bands[c, row] for c in range(3)]
                dil = lam * (d_t[0] + d_p[1])
                put(TT, row, part_s[f, TT, row] + (dil + mu2 * d_t[0]))
                put(TP, row, part_s[f, TP, row] + half * (d_t[1] + d_p[0]))
                put(TR, row, part_s[f, TR, row] + half * d_t[2])
            else:
                dil = lam * d_p[1]
                put(TT, row, part_s[f, TT, row] + dil)
                put(TP, row, part_s[f, TP, row] + half * d_p[0])
                if not last:
                    put(TR, row, part_s[f, TR, row])
            put(PP, row, part_s[f, PP, row] + (dil + mu2 * d_p[1]))
            put(RR, row, part_s[f, RR, row] + dil)
            put(PR, row, part_s[f, PR, row] + half * d_p[2])
        return done

    def edges_stress(step, f):
        phase = 2 * step + 1
        wait_halo(phase, f)
        rims = rim_terms(phase, f)
        done = finish_stress(step, f, BOUNDARY, rims, band_terms(phase, f, (-1, -1, 1)))
        copies = []
        if step < STEPS - 1:
            copies = send_finished(phase, f, 1, rims, stress.at[step + 1, f], lambda c, row: done[TP + c, row])
        return rims, copies

    def materials():
        def body(row, carry):
            ids = ids_in[pl.ds(row, LEV, stride=ROWS), :]
            rho = jnp.zeros((LEV, LANES), F32)
            lam, mu = rho, rho
            for layer in range(16):
                hit = ids == layer
                rho = jnp.where(hit, density_ref[layer], rho)
                lam = jnp.where(hit, lame_ref[layer], lam)
                mu = jnp.where(hit, shear_ref[layer], mu)
            coef[2, row] = step_size * (1.0 / rho)
            coef[3, row] = step_size * lam
            coef[4, row] = (2.0 * step_size) * mu
            return carry

        lax.fori_loop(0, ROWS, body, 0)
        packed = (
            pack_rim(blank, INNER, lambda c, row: coef[2, row] * coef[0, row]),
            pack_rim(
                blank,
                INNER,
                lambda c, row: coef[0, row] * (coef[3, row] + coef[4, row] if c == 1 else 0.5 * coef[4, row]),
            ),
        )
        for kind in range(2):
            for group in range(2):
                coef_rim[kind, group] = packed[kind][group]

    def injection():
        plane = lat_cells * lon_cells
        rows = lax.broadcasted_iota(jnp.int32, (ROWS, LEV, LANES), 0) + lat * ROWS
        levels = lax.broadcasted_iota(jnp.int32, (ROWS, LEV, LANES), 1)
        lanes = lax.broadcasted_iota(jnp.int32, (ROWS, LEV, LANES), 2) + lon * LANES
        cell = levels * plane + rows * lon_cells + lanes
        adds = [jnp.zeros((ROWS, LEV, LANES), F32) for _ in range(STEPS)]
        for s in range(src_ref.shape[0]):
            hit = cell == src_ref[s]
            for step in range(STEPS):
                adds[step] = adds[step] + jnp.where(hit, wave_ref[step, s], 0.0)
        for step in range(STEPS):
            source[step] = adds[step]
        cells = cells_ref[...].reshape(1, -1)
        count = cells.shape[1]
        lev_n = lax.div(cells, plane)
        in_plane = cells - lev_n * plane
        row_n = lax.div(in_plane, lon_cells)
        col_n = in_plane - row_n * lon_cells - lon * LANES
        row_n = row_n - lat * ROWS
        inside = (row_n >= 0) & (row_n < ROWS)
        place_n = jnp.where(inside, row_n * LEV + lev_n, -1)
        index = lax.broadcasted_iota(jnp.int32, (LANES, count), 0)
        lane_hot = jnp.where(index == col_n, 1.0, 0.0).astype(jnp.bfloat16)
        place_hit = index == place_n
        for step in range(STEPS):
            for c in range(3):
                values = resid_ref[c, pl.ds(step, 1)]
                high = values.astype(jnp.bfloat16).astype(F32)
                rest = values - high
                middle = rest.astype(jnp.bfloat16).astype(F32)
                total = None
                for term in (high, middle, rest - middle):
                    left_hot = jnp.where(place_hit, term, 0.0).astype(jnp.bfloat16)
                    piece = lax.dot_general(
                        left_hot, lane_hot, (((1,), (1,)), ((), ())), preferred_element_type=F32
                    )
                    total = piece if total is None else total + piece
                inject[step, c] = total.reshape(ROWS, LEV, LANES)

    started = []
    for f in range(2):
        loads[f].wait()
        unpack_stress(f, range(3), BOUNDARY)
    pl.semaphore_wait(barrier, 4)
    for f in range(2):
        started += send_cols(0, f, stress.at[0, f])
    for f in range(2):
        unpack_stress(f, range(3), INNER)
        unpack_stress(f, range(3, 6), range(ROWS))
        packed = pack_rim(blank, range(ROWS), lambda c, row: stress[0, f, TP + c, 2 + row])
        for group in range(2):
            lon_send[0, f, group] = packed[group]
        started += send_lons(0, f)
    for load in loads[2:]:
        load.wait()
    materials()
    injection()
    for step in range(STEPS):
        for f in range(2):
            local_velocity(step, f)
        rims = []
        for f in range(2):
            rim, copies = edges_velocity(step, f)
            rims.append(rim)
            started += copies
        for f in range(2):
            finish_velocity(step, f, INNER, rims[f])
            local_stress(step, f)
        if step == STEPS - 1:
            for row in range(ROWS):
                density = None
                for s in range(STEPS):
                    for c in range(3):
                        term = vel[s, 0, c, 2 + row] * vel[s, 1, c, 2 + row]
                        density = term if density is None else density + term
                kern_o[pl.ds(row, LEV, stride=ROWS), :] = density
                for f in range(2):
                    for c in range(3):
                        state_o[f, pl.ds(c * (LEV * ROWS) + row, LEV, stride=ROWS), :] = vel[step, f, c, 2 + row]
        rims = []
        for f in range(2):
            rim, copies = edges_stress(step, f)
            rims.append(rim)
            started += copies
        for f in range(2):
            finish_stress(step, f, INNER, rims[f])
    for copy in started:
        copy.wait_send()


def store(state_ref, kern_ref, fwd_out, adj_out, kern_out, sem):
    copies = [
        pltpu.make_async_copy(state_ref.at[0], fwd_out, sem.at[0]),
        pltpu.make_async_copy(state_ref.at[1], adj_out, sem.at[1]),
        pltpu.make_async_copy(kern_ref, kern_out, sem.at[2]),
    ]
    for copy in copies:
        copy.start()
    for copy in copies:
        copy.wait()


def on_device(n_lon, n_lat, forward, adjoint, layer_ids, density, lame, shear, src, wave, cells, resid):
    flat = 9 * LEV * ROWS
    vmem = pl.BlockSpec(memory_space=pltpu.VMEM)
    smem = pl.BlockSpec(memory_space=pltpu.SMEM)
    hbm = pl.BlockSpec(memory_space=pl.ANY)
    phases = 2 * STEPS
    state, kern = pl.pallas_call(
        functools.partial(kernel, n_lon, n_lat),
        out_shape=(pltpu.VMEM((2, flat, LANES), F32), pltpu.VMEM((LEV * ROWS, LANES), F32)),
        in_specs=[hbm, hbm, hbm, smem, smem, smem, smem, smem, vmem, vmem],
        out_specs=(vmem, vmem),
        scratch_shapes=[
            pltpu.VMEM((2, flat, LANES), F32),
            pltpu.VMEM((LEV * ROWS, LANES), jnp.int32),
            pltpu.VMEM((STEPS, 2, 6, ROWS + 4, LEV, LANES), F32),
            pltpu.VMEM((STEPS, 2, 3, ROWS + 4, LEV, LANES), F32),
            pltpu.VMEM((2, 3, ROWS, LEV, LANES), F32),
            pltpu.VMEM((2, 6, ROWS, LEV, LANES), F32),
            pltpu.VMEM((STEPS, 3, ROWS, LEV, LANES), F32),
            pltpu.VMEM((STEPS, ROWS, LEV, LANES), F32),
            pltpu.VMEM((5, ROWS, LEV, LANES), F32),
            pltpu.VMEM((2, 2, LEV, LANES), F32),
            pltpu.VMEM((2, 2, LEV, LANES), F32),
            pltpu.VMEM((phases, 2, 2, 3, 2, LEV, LANES), F32),
            pltpu.VMEM((phases, 2, 2, LEV, LANES), F32),
            pltpu.VMEM((phases, 2, 2, 2, LEV, LANES), F32),
            pltpu.SemaphoreType.DMA((5,)),
            pltpu.SemaphoreType.DMA((phases, 2, 2)),
            pltpu.SemaphoreType.DMA((phases, 2, 2)),
            pltpu.SemaphoreType.DMA((phases, 2, 2)),
            pltpu.SemaphoreType.DMA((phases, 2, 2)),
        ],
        compiler_params=pltpu.CompilerParams(collective_id=0, has_side_effects=True),
        name="elastic_steps",
    )(
        forward.reshape(flat, LANES),
        adjoint.reshape(flat, LANES),
        layer_ids.reshape(LEV * ROWS, LANES),
        density,
        lame,
        shear,
        src,
        wave,
        cells,
        jnp.transpose(resid, (1, 0, 2)),
    )
    fwd, adj, kern = pl.pallas_call(
        store,
        out_shape=(
            jax.ShapeDtypeStruct((flat, LANES), F32),
            jax.ShapeDtypeStruct((flat, LANES), F32),
            jax.ShapeDtypeStruct((LEV * ROWS, LANES), F32),
        ),
        in_specs=[vmem, vmem],
        out_specs=(hbm, hbm, hbm),
        scratch_shapes=[pltpu.SemaphoreType.DMA((3,))],
        compiler_params=pltpu.CompilerParams(vmem_limit_bytes=1 << 20),
        name="store",
    )(pltpu.with_memory_space_constraint(state, pltpu.VMEM), pltpu.with_memory_space_constraint(kern, pltpu.VMEM))
    return fwd.reshape(forward.shape), adj.reshape(adjoint.shape), kern.reshape(layer_ids.shape)


def solution(mesh):
    field = P(None, None, "colat", "lon")
    plane = P(None, "colat", "lon")
    return jax.shard_map(
        functools.partial(on_device, mesh.shape["lon"], mesh.shape["colat"]),
        mesh=mesh,
        in_specs=(field, field, plane) + (P(),) * 7,
        out_specs=(field, field, plane),
        check_vma=False,
    )
```

```python
import functools
import math

import jax
import jax.numpy as jnp
from jax import lax
from jax.experimental import pallas as pl
from jax.experimental.pallas import tpu as pltpu
from jax.sharding import PartitionSpec as P

STEPS = 2
R_INNER = 0.55
COURANT = 0.3
SIN_FLOOR = 0.25
MESH = pl.DeviceIdType.MESH
F32 = jnp.float32

LEV, ROWS, LANES = 8, 16, 128
TT, TR, TP, PP, PR, RR = range(6)
STATE_OF = (3, 7, 6, 4, 8, 5)
CHUNK = 4


def lane_roll(x, shift):
    return pltpu.roll(x, shift % LANES, x.ndim - 1)


def kernel(
    n_lon,
    n_lat,
    fwd_hbm,
    adj_hbm,
    ids_hbm,
    density_ref,
    lame_ref,
    shear_ref,
    src_ref,
    wave_ref,
    cells_ref,
    resid_ref,
    state_o,
    kern_o,
    state_in,
    ids_in,
    stress,
    vel,
    part_v,
    part_s,
    inject,
    source,
    coef,
    part_rim,
    coef_rim,
    col_recv,
    lon_send,
    lon_recv,
    zone,
    zcoef,
    zinject,
    zdensity,
    own_pack,
    own_recv,
    strip_pack,
    strip_mid,
    strip_recv,
    in_sem,
    col_ssem,
    col_rsem,
    lon_ssem,
    lon_rsem,
    zone_ssem,
    zone_rsem,
):
    lon = lax.axis_index("lon")
    lat = lax.axis_index("colat")
    lat_cells, lon_cells = n_lat * ROWS, n_lon * LANES
    is_top = 1 - lax.div(lat + n_lat - 1, n_lat)
    is_bot = lax.div(lat + 1, n_lat)
    left = lax.rem(lon + n_lon - 1, n_lon)
    right = lax.rem(lon + 1, n_lon)
    up = {
        "lon": lax.rem(lon + is_top * (n_lon // 2), n_lon),
        "colat": lat - 1 + is_top,
    }
    down = {
        "lon": lax.rem(lon + is_bot * (n_lon // 2), n_lon),
        "colat": lat + 1 - is_bot,
    }
    to_left = {"lon": left, "colat": lat}
    to_right = {"lon": right, "colat": lat}

    half = n_lon // 2
    place_in_half = lax.rem(lon, half)
    is_e = 1 - lax.div(place_in_half + half - 1, half)
    is_w = lax.div(place_in_half + 1, half)
    at_seam = is_e + is_w
    beside = lax.rem(lon + n_lon - is_e + is_w, n_lon)
    across = {"lon": beside, "colat": lat}
    across_up = {"lon": lax.rem(beside + is_top * half, n_lon), "colat": lat - 1 + is_top}
    across_down = {"lon": lax.rem(beside + is_bot * half, n_lon), "colat": lat + 1 - is_bot}

    barrier = pltpu.get_barrier_semaphore()

    def greet(peer):
        pl.semaphore_signal(barrier, inc=1, device_id=peer, device_id_type=MESH)

    for peer in (up, down, to_left):
        greet(peer)

    @pl.when(is_w == 0)
    def _():
        greet(to_right)

    @pl.when(is_e == 1)
    def _():
        greet(across_up)
        greet(across_down)

    velocity_rows = pl.ds(0, 3 * LEV * ROWS)
    stress_rows = pl.ds(3 * LEV * ROWS, 6 * LEV * ROWS)
    loads = [
        pltpu.make_async_copy(fwd_hbm.at[stress_rows], state_in.at[0, stress_rows], in_sem.at[0]),
        pltpu.make_async_copy(adj_hbm.at[stress_rows], state_in.at[1, stress_rows], in_sem.at[1]),
        pltpu.make_async_copy(ids_hbm, ids_in, in_sem.at[2]),
        pltpu.make_async_copy(fwd_hbm.at[velocity_rows], state_in.at[0, velocity_rows], in_sem.at[3]),
        pltpu.make_async_copy(adj_hbm.at[velocity_rows], state_in.at[1, velocity_rows], in_sem.at[4]),
    ]
    for load in loads:
        load.start()

    theta_step = math.pi / lat_cells
    phi_step = 2.0 * math.pi / lon_cells
    delta_r = (1.0 - R_INNER) / LEV
    step_size = COURANT * SIN_FLOOR * R_INNER * phi_step / 1.6
    level = lax.broadcasted_iota(jnp.int32, (LEV, LANES), 0)
    lane = lax.broadcasted_iota(jnp.int32, (LEV, LANES), 1)
    ir = 1.0 / (R_INNER + (level.astype(F32) + 0.5) * delta_r)
    at = ir * (1.0 / (12.0 * theta_step))
    c_up = jnp.where(level < LEV - 1, 0.5 / delta_r, 0.0).astype(F32)
    c_dn = jnp.where(level > 0, 0.5 / delta_r, 0.0).astype(F32)

    rows3 = lax.broadcasted_iota(jnp.int32, (ROWS, LEV, LANES), 0) + lat * ROWS
    theta = (rows3.astype(F32) + 0.5) * theta_step
    sines = jnp.maximum(jnp.sin(theta), SIN_FLOOR)
    coef[0] = ir[None] / (sines * (12.0 * phi_step))
    coef[1] = jnp.cos(theta) / sines * ir[None]

    for step in range(STEPS):
        for f in range(2):
            zero = jnp.zeros((3, 2, LEV, LANES), F32)
            stress[step, f, 0:3, 0:2] = zero
            stress[step, f, 0:3, ROWS + 2 : ROWS + 4] = zero
            vel[step, f, :, 0:2] = zero
            vel[step, f, :, ROWS + 2 : ROWS + 4] = zero

    BOUNDARY = (0, 1, ROWS - 2, ROWS - 1)
    INNER = tuple(range(2, ROWS - 2))
    INNER_GROUPS = tuple(INNER[i : i + 4] for i in range(0, len(INNER), 4))

    def unpack_stress(f, comps, rows):
        for c in comps:
            first = STATE_OF[c] * (LEV * ROWS)
            values = [state_in[f, pl.ds(first + row, LEV, stride=ROWS), :] for row in rows]
            for row, value in zip(rows, values):
                stress[0, f, c, 2 + row] = value

    def send_cols(phase, f, ref):
        dst_slot = 1 - is_top
        a = pltpu.make_async_remote_copy(
            src_ref=ref.at[0:3, 2:4],
            dst_ref=col_recv.at[phase, f, dst_slot],
            send_sem=col_ssem.at[phase, f, 0],
            recv_sem=col_rsem.at[phase, f, dst_slot],
            device_id=up,
            device_id_type=MESH,
        )
        b = pltpu.make_async_remote_copy(
            src_ref=ref.at[0:3, ROWS : ROWS + 2],
            dst_ref=col_recv.at[phase, f, is_bot],
            send_sem=col_ssem.at[phase, f, 1],
            recv_sem=col_rsem.at[phase, f, is_bot],
            device_id=down,
            device_id_type=MESH,
        )
        a.start()
        b.start()
        return [a, b]

    quad = lax.div(lane, 4)
    spot = lax.rem(lane, 4)

    def pack_rim(base, rows, row_of):
        packed = []
        for group in range(2):
            acc = base[group]
            for slot in range(32):
                c, row = divmod(group * 32 + slot, ROWS)
                if c < 3 and row in rows:
                    acc = jnp.where(quad == slot, lane_roll(row_of(c, row), 4 * slot + 2), acc)
            packed.append(acc)
        return packed

    blank = [jnp.zeros((LEV, LANES), F32)] * 2

    def lon_copy(phase, f, slot):
        return pltpu.make_async_remote_copy(
            src_ref=lon_send.at[phase, f],
            dst_ref=lon_recv.at[phase, f, slot],
            send_sem=lon_ssem.at[phase, f, slot],
            recv_sem=lon_rsem.at[phase, f, slot],
            device_id=(to_right, to_left)[slot],
            device_id_type=MESH,
        )

    def send_lons(phase, f):
        for slot, seam in ((0, is_w), (1, is_e)):

            @pl.when(seam == 0)
            def _():
                lon_copy(phase, f, slot).start()

    def wait_halo(phase, f):
        for slot, seam in ((0, is_e), (1, is_w)):
            pltpu.make_async_remote_copy(
                src_ref=col_recv.at[phase, f, slot],
                dst_ref=col_recv.at[phase, f, slot],
                send_sem=col_ssem.at[phase, f, slot],
                recv_sem=col_rsem.at[phase, f, slot],
                device_id=up,
                device_id_type=MESH,
            ).wait_recv()

            @pl.when(seam == 0)
            def _():
                lon_copy(phase, f, slot).wait_recv()

    def rim_terms(phase, f):
        out = []
        for group in range(2):
            own = lon_send[phase, f, group]
            from_left = jnp.where(is_e == 1, own, lon_recv[phase, f, 0, group])
            from_right = jnp.where(is_w == 1, own, lon_recv[phase, f, 1, group])
            halo = jnp.where(spot < 2, from_left, from_right) - own
            next1, next2 = lane_roll(halo, -1), lane_roll(halo, -2)
            prev1, prev2 = lane_roll(halo, 1), lane_roll(halo, 2)
            term = jnp.where(
                spot == 0,
                -next2,
                jnp.where(spot == 1, 8.0 * next1 - next2, jnp.where(spot == 2, prev2 - 8.0 * prev1, prev2)),
            )
            out.append(term)
        return out

    edge = (lane < 2) | (lane >= LANES - 2)

    def rim_of(terms, c, row):
        k = c * ROWS + row
        return jnp.where(edge, lane_roll(terms[k // 32], -(4 * (k % 32) + 2)), 0.0)

    def band_terms(phase, f, signs):
        flip_top = 1.0 - 2.0 * is_top.astype(F32)
        flip_bot = 1.0 - 2.0 * is_bot.astype(F32)
        terms = {}
        for c in range(3):
            near_top = col_recv[phase, f, 0, c, 1 - is_top]
            far_top = col_recv[phase, f, 0, c, is_top]
            near_bot = col_recv[phase, f, 1, c, is_bot]
            far_bot = col_recv[phase, f, 1, c, 1 - is_bot]
            if signs[c] < 0:
                near_top, far_top = near_top * flip_top, far_top * flip_top
                near_bot, far_bot = near_bot * flip_bot, far_bot * flip_bot
            terms[c, 0] = far_top - 8.0 * near_top
            terms[c, 1] = near_top
            terms[c, ROWS - 2] = -near_bot
            terms[c, ROWS - 1] = 8.0 * near_bot - far_bot
        return terms

    def diff_t(ref, c, r0, n):
        return 8.0 * (ref[c, pl.ds(r0 + 3, n)] - ref[c, pl.ds(r0 + 1, n)]) - (
            ref[c, pl.ds(r0 + 4, n)] - ref[c, pl.ds(r0, n)]
        )

    def diff_p(x):
        return 8.0 * (lane_roll(x, -1) - lane_roll(x, 1)) - (lane_roll(x, -2) - lane_roll(x, 2))

    def diff_r(x):
        return c_up * pltpu.roll(x, LEV - 1, 1) - c_dn * pltpu.roll(x, 1, 1)

    def force_terms(ref, index, cref, r0):
        own = pl.ds(r0, CHUNK)
        ap, cv = cref[0, own], cref[1, own]
        tt, tr, tp, pp, pr, rr = (ref[index[c], pl.ds(r0 + 2, CHUNK)] for c in range(6))
        return (
            at * diff_t(ref, index[TT], r0, CHUNK)
            + ap * diff_p(tp)
            + diff_r(tr)
            + cv * (tt - pp)
            + (3.0 * ir) * tr,
            at * diff_t(ref, index[TP], r0, CHUNK) + ap * diff_p(pp) + diff_r(pr) + 2.0 * cv * tp + (3.0 * ir) * pr,
            at * diff_t(ref, index[TR], r0, CHUNK)
            + ap * diff_p(pr)
            + diff_r(rr)
            + ir * (2.0 * rr - tt - pp)
            + cv * tr,
        )

    def stress_terms(ref, cref, r0):
        own = pl.ds(r0, CHUNK)
        ap, cv = cref[0, own], cref[1, own]
        lam, mu2 = cref[3, own], cref[4, own]
        vt, vp, vr = (ref[c, pl.ds(r0 + 2, CHUNK)] for c in range(3))
        e_tt = at * diff_t(ref, 0, r0, CHUNK) + ir * vr
        e_pp = ap * diff_p(vp) + cv * vt + ir * vr
        e_rr = diff_r(vr)
        e_tp = at * diff_t(ref, 1, r0, CHUNK) - cv * vp + ap * diff_p(vt)
        e_tr = diff_r(vt) - ir * vt + at * diff_t(ref, 2, r0, CHUNK)
        e_pr = diff_r(vp) - ir * vp + ap * diff_p(vr)
        dil = lam * (e_tt + e_pp + e_rr)
        shear = 0.5 * mu2
        return (dil + mu2 * e_tt, shear * e_tr, shear * e_tp, dil + mu2 * e_pp, shear * e_pr, dil + mu2 * e_rr)

    def local_velocity(step, f):
        ref = stress.at[step, f]

        def body(i, carry):
            r0 = i * CHUNK
            own = pl.ds(r0, CHUNK)
            forces = force_terms(ref, range(6), coef, r0)
            scale = coef[2, own]
            for c, force in enumerate(forces):
                value = scale * force
                if step > 0:
                    value = value + vel[step - 1, f, c, pl.ds(r0 + 2, CHUNK)]
                if f == 0:
                    if c == 2:
                        value = value + source[step, own]
                else:
                    value = value + inject[step, c, own]
                part_v[f, c, own] = value
            return carry

        lax.fori_loop(0, ROWS // CHUNK, body, 0)

        if step == 0:
            for c in range(3):
                values = [
                    part_v[f, c, row] + state_in[f, pl.ds(c * (LEV * ROWS) + row, LEV, stride=ROWS), :]
                    for row in range(ROWS)
                ]
                for row in range(ROWS):
                    part_v[f, c, row] = values[row]
        packed = pack_rim(blank, INNER, lambda c, row: part_v[f, c, row])
        for group in range(2):
            part_rim[f, group] = packed[group]

    def send_finished(phase, f, kind, rims, ref, lon_row):
        base = [part_rim[f, group] + coef_rim[kind, group] * rims[group] for group in range(2)]
        packed = pack_rim(base, BOUNDARY, lon_row)
        for group in range(2):
            lon_send[phase + 1, f, group] = packed[group]
        copies = send_cols(phase + 1, f, ref)
        send_lons(phase + 1, f)
        return copies

    def finish_velocity(step, f, rows, rims, bands=None):
        band_of = (TT, TP, TR)
        done = {}
        for row in rows:
            for c in range(3):
                extra = coef[0, row] * rim_of(rims, c, row)
                if bands is not None:
                    extra = extra + at * bands[band_of[c], row]
                done[c, row] = part_v[f, c, row] + coef[2, row] * extra
        for (c, row), value in done.items():
            vel[step, f, c, 2 + row] = value
        return done

    def edges_velocity(step, f):
        phase = 2 * step
        wait_halo(phase, f)
        rims = rim_terms(phase, f)
        done = finish_velocity(step, f, BOUNDARY, rims, band_terms(phase, f, (1, -1, 1)))
        copies = send_finished(phase, f, 0, rims, vel.at[step, f], lambda c, row: done[c, row])
        return rims, copies

    def local_stress(step, f):
        ref = vel.at[step, f]
        old = stress.at[step, f]

        def body(i, carry):
            r0 = i * CHUNK
            own = pl.ds(r0, CHUNK)
            for c, rate in enumerate(stress_terms(ref, coef, r0)):
                part_s[f, c, own] = old[c, pl.ds(r0 + 2, CHUNK)] + rate
            return carry

        lax.fori_loop(0, ROWS // CHUNK, body, 0)
        if step < STEPS - 1:
            packed = pack_rim(blank, INNER, lambda c, row: part_s[f, TP + c, row])
            for group in range(2):
                part_rim[f, group] = packed[group]

    def finish_stress(step, f, rows, rims, bands=None):
        last = step == STEPS - 1
        done = {}

        def put(c, row, value):
            done[c, row] = value

        for row in rows:
            ap, lam, mu2 = coef[0, row], coef[3, row], coef[4, row]
            half = 0.5 * mu2
            d_p = [ap * rim_of(rims, c, row) for c in range(3)]
            if bands is not None:
                d_t = [at * bands[c, row] for c in range(3)]
                dil = lam * (d_t[0] + d_p[1])
                put(TT, row, part_s[f, TT, row] + (dil + mu2 * d_t[0]))
                put(TP, row, part_s[f, TP, row] + half * (d_t[1] + d_p[0]))
                put(TR, row, part_s[f, TR, row] + half * d_t[2])
            else:
                dil = lam * d_p[1]
                put(TT, row, part_s[f, TT, row] + dil)
                put(TP, row, part_s[f, TP, row] + half * d_p[0])
                put(TR, row, part_s[f, TR, row])
            put(PP, row, part_s[f, PP, row] + (dil + mu2 * d_p[1]))
            put(RR, row, part_s[f, RR, row] + dil)
            put(PR, row, part_s[f, PR, row] + half * d_p[2])
        if last:
            finals = {(c, row): zone_or(STATE_OF[c], f, row, value) for (c, row), value in done.items()}
            for (c, row), value in finals.items():
                state_o[f, pl.ds(STATE_OF[c] * (LEV * ROWS) + row, LEV, stride=ROWS), :] = value
        else:
            for (c, row), value in done.items():
                stress[step + 1, f, c, 2 + row] = value
        return done

    def edges_stress(step, f):
        phase = 2 * step + 1
        wait_halo(phase, f)
        rims = rim_terms(phase, f)
        done = finish_stress(step, f, BOUNDARY, rims, band_terms(phase, f, (-1, -1, 1)))
        copies = []
        if step < STEPS - 1:
            copies = send_finished(phase, f, 1, rims, stress.at[step + 1, f], lambda c, row: done[TP + c, row])
        return rims, copies

    def materials():
        def body(i, carry):
            own = pl.ds(i * CHUNK, CHUNK)
            ids = jnp.stack([ids_in[pl.ds(i * CHUNK + k, LEV, stride=ROWS), :] for k in range(CHUNK)])
            rho = jnp.zeros((CHUNK, LEV, LANES), F32)
            lam, mu = rho, rho
            for layer in range(16):
                hit = ids == layer
                rho = jnp.where(hit, density_ref[layer], rho)
                lam = jnp.where(hit, lame_ref[layer], lam)
                mu = jnp.where(hit, shear_ref[layer], mu)
            coef[2, own] = step_size * (1.0 / rho)
            coef[3, own] = step_size * lam
            coef[4, own] = (2.0 * step_size) * mu
            return carry

        lax.fori_loop(0, ROWS // CHUNK, body, 0)
        packed = (
            pack_rim(blank, INNER, lambda c, row: coef[2, row] * coef[0, row]),
            pack_rim(
                blank,
                INNER,
                lambda c, row: coef[0, row] * (coef[3, row] + coef[4, row] if c == 1 else 0.5 * coef[4, row]),
            ),
        )
        for kind in range(2):
            for group in range(2):
                coef_rim[kind, group] = packed[kind][group]

    def injection():
        plane = lat_cells * lon_cells
        rows = lax.broadcasted_iota(jnp.int32, (ROWS, LEV, LANES), 0) + lat * ROWS
        levels = lax.broadcasted_iota(jnp.int32, (ROWS, LEV, LANES), 1)
        lanes = lax.broadcasted_iota(jnp.int32, (ROWS, LEV, LANES), 2) + lon * LANES
        cell = levels * plane + rows * lon_cells + lanes
        adds = [jnp.zeros((ROWS, LEV, LANES), F32) for _ in range(STEPS)]
        for s in range(src_ref.shape[0]):
            hit = cell == src_ref[s]
            for step in range(STEPS):
                adds[step] = adds[step] + jnp.where(hit, wave_ref[step, s], 0.0)
        for step in range(STEPS):
            source[step] = adds[step]
        cells = cells_ref[...].reshape(1, -1)
        count = cells.shape[1]
        lev_n = lax.div(cells, plane)
        in_plane = cells - lev_n * plane
        row_n = lax.div(in_plane, lon_cells)
        col_n = in_plane - row_n * lon_cells - lon * LANES
        row_n = row_n - lat * ROWS
        inside = (row_n >= 0) & (row_n < ROWS)
        place_n = jnp.where(inside, row_n * LEV + lev_n, -1)
        index = lax.broadcasted_iota(jnp.int32, (LANES, count), 0)
        lane_hot = jnp.where(index == col_n, 1.0, 0.0).astype(jnp.bfloat16)
        place_hit = index == place_n
        for step in range(STEPS):
            for c in range(3):
                values = resid_ref[c, pl.ds(step, 1)]
                high = values.astype(jnp.bfloat16).astype(F32)
                rest = values - high
                middle = rest.astype(jnp.bfloat16).astype(F32)
                total = None
                for term in (high, middle, rest - middle):
                    left_hot = jnp.where(place_hit, term, 0.0).astype(jnp.bfloat16)
                    piece = lax.dot_general(
                        left_hot, lane_hot, (((1,), (1,)), ((), ())), preferred_element_type=F32
                    )
                    total = piece if total is None else total + piece
                inject[step, c] = total.reshape(ROWS, LEV, LANES)

    ZROWS = 2 * ROWS
    side = lax.rem(lane, 64)
    own_at = 16 * is_e
    strip_at = 8 + 8 * is_e
    own_side = (side >= own_at) & (side < own_at + 16)
    own_slot = lax.div(lax.rem(lane - own_at + 64, 64), 16)
    strip_slot = lax.div(lax.rem(lane - strip_at + 64, 64), 8)

    def pack_channel(ch, rows_of):
        strips = [jnp.zeros((LEV, LANES), F32)] * 2
        owns = [[jnp.zeros((LEV, LANES), F32)] * 2 for _ in range(2)]
        window = []
        for row in range(ROWS):
            h, q = divmod(row, 8)
            fwd, adj = rows_of(row)
            both = jnp.where(lane < 64, lane_roll(fwd, 16), lane_roll(adj, 80))
            window.append(both)
            moved = lane_roll(both, 8 * q) if q else both
            strips[h] = jnp.where(strip_slot == q, moved, strips[h])
            moved = lane_roll(both, 16 * (q % 4)) if q % 4 else both
            owns[h][q // 4] = jnp.where(own_slot == q % 4, moved, owns[h][q // 4])
        for row in range(ROWS):
            zone[ch, 2 + 8 + row] = window[row]
        for h in range(2):
            strip_pack[h, ch] = strips[h]
            for g in range(2):
                own_pack[h, ch, g] = owns[h][g]

    def zone_pack_strips():
        def body(ch, carry):
            def rows_of(row):
                rows = pl.ds(ch * (LEV * ROWS) + row, LEV, stride=ROWS)
                return state_in[0, rows, :], state_in[1, rows, :]

            pack_channel(ch, rows_of)
            return carry

        lax.fori_loop(0, 9, body, 0)
        pack_channel(9, lambda row: (ids_in[pl.ds(row, LEV, stride=ROWS), :].astype(F32),) * 2)

    def zone_copy(kind):
        src, dst, slot, peer = (
            (own_pack.at[0], own_recv.at[1 - is_top], 1 - is_top, up),
            (own_pack.at[1], own_recv.at[is_bot], is_bot, down),
            (strip_pack, strip_mid, 2, across),
            (strip_pack.at[0], strip_recv.at[1 - is_top], 4 - is_top, across_up),
            (strip_pack.at[1], strip_recv.at[is_bot], 3 + is_bot, across_down),
        )[kind]
        return pltpu.make_async_remote_copy(
            src_ref=src,
            dst_ref=dst,
            send_sem=zone_ssem.at[kind],
            recv_sem=zone_rsem.at[slot],
            device_id=peer,
            device_id_type=MESH,
        )

    def zone_wait(slot):
        ref = (own_recv.at[0], own_recv.at[1], strip_mid, strip_recv.at[0], strip_recv.at[1])[slot]
        pltpu.make_async_remote_copy(
            src_ref=ref,
            dst_ref=ref,
            send_sem=zone_ssem.at[slot],
            recv_sem=zone_rsem.at[slot],
            device_id=up,
            device_id_type=MESH,
        ).wait_recv()

    def zone_start():
        zone_pack_strips()

        @pl.when(is_w == 1)
        def _():
            for kind in (2, 3, 4):
                zone_copy(kind).start()

    def zone_start_own():
        zone_copy(0).start()
        zone_copy(1).start()

    def zone_receive():
        for slot in (2, 3, 4):
            zone_wait(slot)

        @pl.when(is_e == 1)
        def _():
            for kind in (2, 3, 4):
                zone_copy(kind).start()

        for slot in (0, 1):
            zone_wait(slot)
        flips = (1.0 - 2.0 * is_top.astype(F32), 1.0 - 2.0 * is_bot.astype(F32))

        def body(ch, carry):
            middle = []
            for row in range(ROWS):
                h, q = divmod(row, 8)
                strip = lane_roll(strip_mid[h, ch], -8 * q) if q else strip_mid[h, ch]
                middle.append(jnp.where(own_side, zone[ch, 2 + 8 + row], strip))
            for row in range(ROWS):
                zone[ch, 2 + 8 + row] = middle[row]
            turns = (ch < 2) | (ch == 7) | (ch == 8)
            for slot, pole, first in ((0, is_top, 0), (1, is_bot, 24)):
                flip = jnp.where(turns, flips[slot], 1.0)
                values = []
                for q in range(8):
                    own = own_recv[slot, ch, q // 4]
                    own = lane_roll(own, -16 * (q % 4)) if q % 4 else own
                    strip = strip_recv[slot, ch]
                    strip = lane_roll(strip, -8 * q) if q else strip
                    values.append(jnp.where(own_side, own, strip) * flip)
                for q in range(8):
                    zone[ch, 2 + first + q] = jnp.where(pole == 1, values[7 - q], values[q])
            return carry

        lax.fori_loop(0, 10, body, 0)

    def zone_wait_sends():
        for kind in range(5):
            zone_copy(kind).wait_send()

    def zone_cells():
        row = lax.broadcasted_iota(jnp.int32, (ZROWS, LEV, LANES), 0) + (lat * ROWS - 8)
        col = lax.broadcasted_iota(jnp.int32, (ZROWS, LEV, LANES), 2) + (lon * LANES + 112 - 128 * is_e + lon_cells)
        turned = (row < 0) | (row >= lat_cells)
        row = jnp.where(row < 0, -1 - row, jnp.where(row >= lat_cells, 2 * lat_cells - 1 - row, row))
        col = lax.rem(col + jnp.where(turned, lon_cells // 2, 0), lon_cells)
        return row, col

    def zone_metrics():
        row = lax.broadcasted_iota(jnp.int32, (ZROWS, LEV, LANES), 0) + (lat * ROWS - 8)
        beyond = (row < 0) | (row >= lat_cells)
        row = jnp.where(row < 0, -1 - row, jnp.where(row >= lat_cells, 2 * lat_cells - 1 - row, row))
        theta = (row.astype(F32) + 0.5) * theta_step
        sines = jnp.maximum(jnp.sin(theta), SIN_FLOOR) * jnp.where(beyond, -1.0, 1.0)
        zcoef[0] = ir[None] / (sines * (12.0 * phi_step))
        zcoef[1] = jnp.cos(theta) / sines * ir[None]

    def zone_materials():
        def body(i, carry):
            row = pl.ds(2 + i * CHUNK, CHUNK)
            ids = zone[9, pl.ds(4 + i * CHUNK, CHUNK)].astype(jnp.int32)
            rho = jnp.ones((CHUNK, LEV, LANES), F32)
            lam, mu = rho, rho
            for layer in range(16):
                hit = ids == layer
                rho = jnp.where(hit, density_ref[layer], rho)
                lam = jnp.where(hit, lame_ref[layer], lam)
                mu = jnp.where(hit, shear_ref[layer], mu)
            zcoef[2, row] = step_size * (1.0 / rho)
            zcoef[3, row] = step_size * lam
            zcoef[4, row] = (2.0 * step_size) * mu
            return carry

        lax.fori_loop(0, (ZROWS - 4) // CHUNK, body, 0)

    def zone_injection():
        plane = lat_cells * lon_cells
        row, col = zone_cells()
        level3 = lax.broadcasted_iota(jnp.int32, (ZROWS, LEV, LANES), 1)
        lane3 = lax.broadcasted_iota(jnp.int32, (ZROWS, LEV, LANES), 2)
        cell = jnp.where(lane3 < 32, level3 * plane + row * lon_cells + col, -1)
        cells = cells_ref[...].reshape(1, -1)
        count = cells.shape[1]
        lev_n = lax.div(cells, plane)
        in_plane = cells - lev_n * plane
        row_n = lax.div(in_plane, lon_cells)
        first = lon * LANES + 112 - 128 * is_e
        col_n = lax.rem(in_plane - row_n * lon_cells - first + 2 * lon_cells, lon_cells)
        over_n = lax.rem(col_n + lon_cells // 2, lon_cells)
        straight = row_n - (lat * ROWS - 8)
        turned = jnp.where(row_n < 8, 7 - row_n, lat_cells - 1 - row_n + 24)
        can_turn = ((row_n < 8) & (is_top == 1)) | ((row_n >= lat_cells - 8) & (is_bot == 1))
        is_turned = can_turn & (over_n < 32)
        is_straight = (straight >= 0) & (straight < ZROWS) & (col_n < 32)
        zrow_n = jnp.where(is_turned, turned, straight)
        zcol_n = jnp.where(is_turned, over_n, col_n) + 64
        place_n = jnp.where(is_turned | is_straight, zrow_n * LEV + lev_n, -1)
        sign_n = jnp.where(is_turned, -1.0, 1.0)
        index = lax.broadcasted_iota(jnp.int32, (LANES, count), 0)
        lane_hot = jnp.where(index == zcol_n, 1.0, 0.0).astype(jnp.bfloat16)
        for part in range(2):
            place_hit = index + part * LANES == place_n
            for step in range(STEPS):
                for c in range(3):
                    values = resid_ref[c, pl.ds(step, 1)]
                    if c < 2:
                        values = values * sign_n
                    high = values.astype(jnp.bfloat16).astype(F32)
                    rest = values - high
                    middle = rest.astype(jnp.bfloat16).astype(F32)
                    total = None
                    for term in (high, middle, rest - middle):
                        left_hot = jnp.where(place_hit, term, 0.0).astype(jnp.bfloat16)
                        piece = lax.dot_general(
                            left_hot, lane_hot, (((1,), (1,)), ((), ())), preferred_element_type=F32
                        )
                        total = piece if total is None else total + piece
                    zinject[step, c, part * ROWS : (part + 1) * ROWS] = total.reshape(ROWS, LEV, LANES)
        adds = [jnp.zeros((ZROWS, LEV, LANES), F32) for _ in range(STEPS)]
        for s in range(src_ref.shape[0]):
            hit = cell == src_ref[s]
            for step in range(STEPS):
                adds[step] = adds[step] + jnp.where(hit, wave_ref[step, s], 0.0)
        for step in range(STEPS):
            zinject[step, 2] += adds[step]

    def zone_steps():
        for step in range(STEPS):

            def velocity_body(i, carry):
                r0 = 2 + 4 * step + i * CHUNK
                own = pl.ds(r0, CHUNK)
                scale = zcoef[2, own]
                for c, force in enumerate(force_terms(zone, STATE_OF, zcoef, r0)):
                    zone[c, pl.ds(r0 + 2, CHUNK)] += scale * force + zinject[step, c, own]
                return carry

            lax.fori_loop(0, 7 - 2 * step, velocity_body, 0)
            density = None
            for c in range(3):
                new = zone[c, 2 + 8 : 2 + 8 + ROWS]
                term = new * lane_roll(new, 64)
                density = term if density is None else density + term
            zdensity[...] = density if step == 0 else zdensity[...] + density

            def stress_body(i, carry):
                r0 = 4 + 4 * step + i * CHUNK
                for c, rate in enumerate(stress_terms(zone, zcoef, r0)):
                    zone[STATE_OF[c], pl.ds(r0 + 2, CHUNK)] += rate
                return carry

            lax.fori_loop(0, 6 - 2 * step, stress_body, 0)

    seam_side = (lane >= LANES * (1 - is_e) - 8 * is_w) & (lane < LANES - (LANES - 8) * is_e)

    def zone_or(ch, f, row, value):
        return jnp.where(seam_side, lane_roll(zone[ch, 2 + 8 + row], -16 - 64 * f), value)

    started = []
    for f in range(2):
        loads[f].wait()
        unpack_stress(f, range(3), BOUNDARY)
    pl.semaphore_wait(barrier, 4 - is_e + 2 * is_w)
    for f in range(2):
        started += send_cols(0, f, stress.at[0, f])
    for f in range(2):
        unpack_stress(f, range(3), INNER)
        unpack_stress(f, range(3, 6), range(ROWS))
        packed = pack_rim(blank, range(ROWS), lambda c, row: stress[0, f, TP + c, 2 + row])
        for group in range(2):
            lon_send[0, f, group] = packed[group]
        send_lons(0, f)
    for load in loads[2:]:
        load.wait()

    @pl.when(is_w == 1)
    def _():
        zone_start()

    materials()
    injection()
    for step in range(STEPS):
        for f in range(2):
            local_velocity(step, f)
        if step == 1:

            @pl.when(at_seam == 1)
            def _():
                zone_injection()

        rims = []
        for f in range(2):
            rim, copies = edges_velocity(step, f)
            rims.append(rim)
            started += copies
        for f in range(2):
            for rows in INNER_GROUPS:
                finish_velocity(step, f, rows, rims[f])
            local_stress(step, f)
        if step == 0:

            @pl.when(is_e == 1)
            def _():
                zone_start()

            @pl.when(at_seam == 1)
            def _():
                zone_start_own()
                zone_metrics()

        if step == STEPS - 1:

            @pl.when(at_seam == 1)
            def _():
                zone_receive()
                zone_materials()
                zone_steps()

            densities = []
            for row in range(ROWS):
                density = None
                for s in range(STEPS):
                    for c in range(3):
                        term = vel[s, 0, c, 2 + row] * vel[s, 1, c, 2 + row]
                        density = term if density is None else density + term
                densities.append(jnp.where(seam_side, lane_roll(zdensity[row], -16), density))
            for row in range(ROWS):
                kern_o[pl.ds(row, LEV, stride=ROWS), :] = densities[row]
            for f in range(2):
                for c in range(3):
                    values = [zone_or(c, f, row, vel[step, f, c, 2 + row]) for row in range(ROWS)]
                    for row in range(ROWS):
                        state_o[f, pl.ds(c * (LEV * ROWS) + row, LEV, stride=ROWS), :] = values[row]
        rims = []
        for f in range(2):
            rim, copies = edges_stress(step, f)
            rims.append(rim)
            started += copies
        for f in range(2):
            for rows in INNER_GROUPS:
                finish_stress(step, f, rows, rims[f])

    for copy in started:
        copy.wait_send()
    for phase in range(2 * STEPS):
        for f in range(2):
            for slot, seam in ((0, is_w), (1, is_e)):

                @pl.when(seam == 0)
                def _():
                    lon_copy(phase, f, slot).wait_send()

    @pl.when(at_seam == 1)
    def _():
        zone_wait_sends()


def store(state_ref, kern_ref, fwd_out, adj_out, kern_out, sem):
    copies = [
        pltpu.make_async_copy(state_ref.at[0], fwd_out, sem.at[0]),
        pltpu.make_async_copy(state_ref.at[1], adj_out, sem.at[1]),
        pltpu.make_async_copy(kern_ref, kern_out, sem.at[2]),
    ]
    for copy in copies:
        copy.start()
    for copy in copies:
        copy.wait()


def on_device(n_lon, n_lat, forward, adjoint, layer_ids, density, lame, shear, src, wave, cells, resid):
    flat = 9 * LEV * ROWS
    vmem = pl.BlockSpec(memory_space=pltpu.VMEM)
    smem = pl.BlockSpec(memory_space=pltpu.SMEM)
    hbm = pl.BlockSpec(memory_space=pl.ANY)
    phases = 2 * STEPS
    state, kern = pl.pallas_call(
        functools.partial(kernel, n_lon, n_lat),
        out_shape=(pltpu.VMEM((2, flat, LANES), F32), pltpu.VMEM((LEV * ROWS, LANES), F32)),
        in_specs=[hbm, hbm, hbm, smem, smem, smem, smem, smem, vmem, vmem],
        out_specs=(vmem, vmem),
        scratch_shapes=[
            pltpu.VMEM((2, flat, LANES), F32),
            pltpu.VMEM((LEV * ROWS, LANES), jnp.int32),
            pltpu.VMEM((STEPS, 2, 6, ROWS + 4, LEV, LANES), F32),
            pltpu.VMEM((STEPS, 2, 3, ROWS + 4, LEV, LANES), F32),
            pltpu.VMEM((2, 3, ROWS, LEV, LANES), F32),
            pltpu.VMEM((2, 6, ROWS, LEV, LANES), F32),
            pltpu.VMEM((STEPS, 3, ROWS, LEV, LANES), F32),
            pltpu.VMEM((STEPS, ROWS, LEV, LANES), F32),
            pltpu.VMEM((5, ROWS, LEV, LANES), F32),
            pltpu.VMEM((2, 2, LEV, LANES), F32),
            pltpu.VMEM((2, 2, LEV, LANES), F32),
            pltpu.VMEM((phases, 2, 2, 3, 2, LEV, LANES), F32),
            pltpu.VMEM((phases, 2, 2, LEV, LANES), F32),
            pltpu.VMEM((phases, 2, 2, 2, LEV, LANES), F32),
            pltpu.VMEM((10, 2 * ROWS + 4, LEV, LANES), F32),
            pltpu.VMEM((5, 2 * ROWS, LEV, LANES), F32),
            pltpu.VMEM((STEPS, 3, 2 * ROWS, LEV, LANES), F32),
            pltpu.VMEM((ROWS, LEV, LANES), F32),
            pltpu.VMEM((2, 10, 2, LEV, LANES), F32),
            pltpu.VMEM((2, 10, 2, LEV, LANES), F32),
            pltpu.VMEM((2, 10, LEV, LANES), F32),
            pltpu.VMEM((2, 10, LEV, LANES), F32),
            pltpu.VMEM((2, 10, LEV, LANES), F32),
            pltpu.SemaphoreType.DMA((5,)),
            pltpu.SemaphoreType.DMA((phases, 2, 2)),
            pltpu.SemaphoreType.DMA((phases, 2, 2)),
            pltpu.SemaphoreType.DMA((phases, 2, 2)),
            pltpu.SemaphoreType.DMA((phases, 2, 2)),
            pltpu.SemaphoreType.DMA((5,)),
            pltpu.SemaphoreType.DMA((5,)),
        ],
        compiler_params=pltpu.CompilerParams(collective_id=0, has_side_effects=True),
        name="elastic_steps",
    )(
        forward.reshape(flat, LANES),
        adjoint.reshape(flat, LANES),
        layer_ids.reshape(LEV * ROWS, LANES),
        density,
        lame,
        shear,
        src,
        wave,
        cells,
        jnp.transpose(resid, (1, 0, 2)),
    )
    fwd, adj, kern = pl.pallas_call(
        store,
        out_shape=(
            jax.ShapeDtypeStruct((flat, LANES), F32),
            jax.ShapeDtypeStruct((flat, LANES), F32),
            jax.ShapeDtypeStruct((LEV * ROWS, LANES), F32),
        ),
        in_specs=[vmem, vmem],
        out_specs=(hbm, hbm, hbm),
        scratch_shapes=[pltpu.SemaphoreType.DMA((3,))],
        compiler_params=pltpu.CompilerParams(vmem_limit_bytes=1 << 20),
        name="store",
    )(pltpu.with_memory_space_constraint(state, pltpu.VMEM), pltpu.with_memory_space_constraint(kern, pltpu.VMEM))
    return fwd.reshape(forward.shape), adj.reshape(adjoint.shape), kern.reshape(layer_ids.shape)


def solution(mesh):
    field = P(None, None, "colat", "lon")
    plane = P(None, "colat", "lon")
    return jax.shard_map(
        functools.partial(on_device, mesh.shape["lon"], mesh.shape["colat"]),
        mesh=mesh,
        in_specs=(field, field, plane) + (P(),) * 7,
        out_specs=(field, field, plane),
        check_vma=False,
    )
```

```python
import functools
import math

import jax
import jax.numpy as jnp
from jax import lax
from jax.experimental import pallas as pl
from jax.experimental.pallas import tpu as pltpu
from jax.sharding import PartitionSpec as P

STEPS = 2
R_INNER = 0.55
COURANT = 0.3
SIN_FLOOR = 0.25
MESH = pl.DeviceIdType.MESH
F32 = jnp.float32

LEV, ROWS, LANES = 8, 16, 128
TT, TR, TP, PP, PR, RR = range(6)
STATE_OF = (3, 7, 6, 4, 8, 5)
CHUNK = 4


def lane_roll(x, shift):
    return pltpu.roll(x, shift % LANES, x.ndim - 1)


def kernel(
    n_lon,
    n_lat,
    fwd_hbm,
    adj_hbm,
    ids_hbm,
    density_ref,
    lame_ref,
    shear_ref,
    src_ref,
    wave_ref,
    cells_ref,
    resid_ref,
    state_o,
    kern_o,
    state_in,
    ids_in,
    stress,
    vel,
    part_v,
    part_s,
    inject,
    source,
    coef,
    part_rim,
    coef_rim,
    col_recv,
    lon_send,
    lon_recv,
    zone,
    zcoef,
    zinject,
    zdensity,
    own_pack,
    own_recv,
    strip_pack,
    strip_mid,
    strip_recv,
    in_sem,
    col_ssem,
    col_rsem,
    lon_ssem,
    lon_rsem,
    zone_ssem,
    zone_rsem,
):
    lon = lax.axis_index("lon")
    lat = lax.axis_index("colat")
    lat_cells, lon_cells = n_lat * ROWS, n_lon * LANES
    is_top = 1 - lax.div(lat + n_lat - 1, n_lat)
    is_bot = lax.div(lat + 1, n_lat)
    left = lax.rem(lon + n_lon - 1, n_lon)
    right = lax.rem(lon + 1, n_lon)
    up = {
        "lon": lax.rem(lon + is_top * (n_lon // 2), n_lon),
        "colat": lat - 1 + is_top,
    }
    down = {
        "lon": lax.rem(lon + is_bot * (n_lon // 2), n_lon),
        "colat": lat + 1 - is_bot,
    }
    to_left = {"lon": left, "colat": lat}
    to_right = {"lon": right, "colat": lat}

    half = n_lon // 2
    place_in_half = lax.rem(lon, half)
    is_e = 1 - lax.div(place_in_half + half - 1, half)
    is_w = lax.div(place_in_half + 1, half)
    at_seam = is_e + is_w
    beside = lax.rem(lon + n_lon - is_e + is_w, n_lon)
    across = {"lon": beside, "colat": lat}
    across_up = {"lon": lax.rem(beside + is_top * half, n_lon), "colat": lat - 1 + is_top}
    across_down = {"lon": lax.rem(beside + is_bot * half, n_lon), "colat": lat + 1 - is_bot}

    barrier = pltpu.get_barrier_semaphore()

    def greet(peer):
        pl.semaphore_signal(barrier, inc=1, device_id=peer, device_id_type=MESH)

    for peer in (up, down, to_left):
        greet(peer)

    @pl.when(is_w == 0)
    def _():
        greet(to_right)

    @pl.when(is_e == 1)
    def _():
        greet(across_up)
        greet(across_down)

    velocity_rows = pl.ds(0, 3 * LEV * ROWS)
    stress_rows = pl.ds(3 * LEV * ROWS, 6 * LEV * ROWS)
    loads = [
        pltpu.make_async_copy(fwd_hbm.at[stress_rows], state_in.at[0, stress_rows], in_sem.at[0]),
        pltpu.make_async_copy(adj_hbm.at[stress_rows], state_in.at[1, stress_rows], in_sem.at[1]),
        pltpu.make_async_copy(ids_hbm, ids_in, in_sem.at[2]),
        pltpu.make_async_copy(fwd_hbm.at[velocity_rows], state_in.at[0, velocity_rows], in_sem.at[3]),
        pltpu.make_async_copy(adj_hbm.at[velocity_rows], state_in.at[1, velocity_rows], in_sem.at[4]),
    ]
    for load in loads:
        load.start()

    theta_step = math.pi / lat_cells
    phi_step = 2.0 * math.pi / lon_cells
    delta_r = (1.0 - R_INNER) / LEV
    step_size = COURANT * SIN_FLOOR * R_INNER * phi_step / 1.6
    level = lax.broadcasted_iota(jnp.int32, (LEV, LANES), 0)
    lane = lax.broadcasted_iota(jnp.int32, (LEV, LANES), 1)
    ir = 1.0 / (R_INNER + (level.astype(F32) + 0.5) * delta_r)
    at = ir * (1.0 / (12.0 * theta_step))
    c_up = jnp.where(level < LEV - 1, 0.5 / delta_r, 0.0).astype(F32)
    c_dn = jnp.where(level > 0, 0.5 / delta_r, 0.0).astype(F32)

    rows3 = lax.broadcasted_iota(jnp.int32, (ROWS, LEV, LANES), 0) + lat * ROWS
    theta = (rows3.astype(F32) + 0.5) * theta_step
    sines = jnp.maximum(jnp.sin(theta), SIN_FLOOR)
    coef[0] = ir[None] / (sines * (12.0 * phi_step))
    coef[1] = jnp.cos(theta) / sines * ir[None]

    for step in range(STEPS):
        for f in range(2):
            zero = jnp.zeros((3, 2, LEV, LANES), F32)
            stress[step, f, 0:3, 0:2] = zero
            stress[step, f, 0:3, ROWS + 2 : ROWS + 4] = zero
            vel[step, f, :, 0:2] = zero
            vel[step, f, :, ROWS + 2 : ROWS + 4] = zero

    BOUNDARY = (0, 1, ROWS - 2, ROWS - 1)
    INNER = tuple(range(2, ROWS - 2))
    INNER_GROUPS = tuple(INNER[i : i + 4] for i in range(0, len(INNER), 4))

    def unpack_stress(f, comps, rows):
        for c in comps:
            first = STATE_OF[c] * (LEV * ROWS)
            values = [state_in[f, pl.ds(first + row, LEV, stride=ROWS), :] for row in rows]
            for row, value in zip(rows, values):
                stress[0, f, c, 2 + row] = value

    def send_cols(phase, f, ref):
        dst_slot = 1 - is_top
        a = pltpu.make_async_remote_copy(
            src_ref=ref.at[0:3, 2:4],
            dst_ref=col_recv.at[phase, f, dst_slot],
            send_sem=col_ssem.at[phase, f, 0],
            recv_sem=col_rsem.at[phase, f, dst_slot],
            device_id=up,
            device_id_type=MESH,
        )
        b = pltpu.make_async_remote_copy(
            src_ref=ref.at[0:3, ROWS : ROWS + 2],
            dst_ref=col_recv.at[phase, f, is_bot],
            send_sem=col_ssem.at[phase, f, 1],
            recv_sem=col_rsem.at[phase, f, is_bot],
            device_id=down,
            device_id_type=MESH,
        )
        a.start()
        b.start()
        return [a, b]

    quad = lax.div(lane, 4)
    spot = lax.rem(lane, 4)

    def pack_rim(base, rows, row_of):
        packed = []
        for group in range(2):
            acc = base[group]
            for slot in range(32):
                c, row = divmod(group * 32 + slot, ROWS)
                if c < 3 and row in rows:
                    acc = jnp.where(quad == slot, lane_roll(row_of(c, row), 4 * slot + 2), acc)
            packed.append(acc)
        return packed

    blank = [jnp.zeros((LEV, LANES), F32)] * 2

    def lon_copy(phase, f, slot):
        return pltpu.make_async_remote_copy(
            src_ref=lon_send.at[phase, f],
            dst_ref=lon_recv.at[phase, f, slot],
            send_sem=lon_ssem.at[phase, f, slot],
            recv_sem=lon_rsem.at[phase, f, slot],
            device_id=(to_right, to_left)[slot],
            device_id_type=MESH,
        )

    def send_lons(phase, f):
        for slot, seam in ((0, is_w), (1, is_e)):

            @pl.when(seam == 0)
            def _():
                lon_copy(phase, f, slot).start()

    def wait_halo(phase, f):
        for slot, seam in ((0, is_e), (1, is_w)):
            pltpu.make_async_remote_copy(
                src_ref=col_recv.at[phase, f, slot],
                dst_ref=col_recv.at[phase, f, slot],
                send_sem=col_ssem.at[phase, f, slot],
                recv_sem=col_rsem.at[phase, f, slot],
                device_id=up,
                device_id_type=MESH,
            ).wait_recv()

            @pl.when(seam == 0)
            def _():
                lon_copy(phase, f, slot).wait_recv()

    def rim_terms(phase, f):
        out = []
        for group in range(2):
            own = lon_send[phase, f, group]
            from_left = jnp.where(is_e == 1, own, lon_recv[phase, f, 0, group])
            from_right = jnp.where(is_w == 1, own, lon_recv[phase, f, 1, group])
            halo = jnp.where(spot < 2, from_left, from_right) - own
            next1, next2 = lane_roll(halo, -1), lane_roll(halo, -2)
            prev1, prev2 = lane_roll(halo, 1), lane_roll(halo, 2)
            term = jnp.where(
                spot == 0,
                -next2,
                jnp.where(spot == 1, 8.0 * next1 - next2, jnp.where(spot == 2, prev2 - 8.0 * prev1, prev2)),
            )
            out.append(term)
        return out

    edge = (lane < 2) | (lane >= LANES - 2)

    def rim_of(terms, c, row):
        k = c * ROWS + row
        return jnp.where(edge, lane_roll(terms[k // 32], -(4 * (k % 32) + 2)), 0.0)

    def band_terms(phase, f, signs):
        flip_top = 1.0 - 2.0 * is_top.astype(F32)
        flip_bot = 1.0 - 2.0 * is_bot.astype(F32)
        terms = {}
        for c in range(3):
            near_top = col_recv[phase, f, 0, c, 1 - is_top]
            far_top = col_recv[phase, f, 0, c, is_top]
            near_bot = col_recv[phase, f, 1, c, is_bot]
            far_bot = col_recv[phase, f, 1, c, 1 - is_bot]
            if signs[c] < 0:
                near_top, far_top = near_top * flip_top, far_top * flip_top
                near_bot, far_bot = near_bot * flip_bot, far_bot * flip_bot
            terms[c, 0] = far_top - 8.0 * near_top
            terms[c, 1] = near_top
            terms[c, ROWS - 2] = -near_bot
            terms[c, ROWS - 1] = 8.0 * near_bot - far_bot
        return terms

    def diff_t(ref, c, r0, n):
        return 8.0 * (ref[c, pl.ds(r0 + 3, n)] - ref[c, pl.ds(r0 + 1, n)]) - (
            ref[c, pl.ds(r0 + 4, n)] - ref[c, pl.ds(r0, n)]
        )

    def diff_p(x):
        return 8.0 * (lane_roll(x, -1) - lane_roll(x, 1)) - (lane_roll(x, -2) - lane_roll(x, 2))

    def diff_r(x):
        return c_up * pltpu.roll(x, LEV - 1, 1) - c_dn * pltpu.roll(x, 1, 1)

    def force_terms(ref, index, cref, r0):
        own = pl.ds(r0, CHUNK)
        ap, cv = cref[0, own], cref[1, own]
        tt, tr, tp, pp, pr, rr = (ref[index[c], pl.ds(r0 + 2, CHUNK)] for c in range(6))
        return (
            at * diff_t(ref, index[TT], r0, CHUNK)
            + ap * diff_p(tp)
            + diff_r(tr)
            + cv * (tt - pp)
            + (3.0 * ir) * tr,
            at * diff_t(ref, index[TP], r0, CHUNK) + ap * diff_p(pp) + diff_r(pr) + 2.0 * cv * tp + (3.0 * ir) * pr,
            at * diff_t(ref, index[TR], r0, CHUNK)
            + ap * diff_p(pr)
            + diff_r(rr)
            + ir * (2.0 * rr - tt - pp)
            + cv * tr,
        )

    def stress_terms(ref, cref, r0):
        own = pl.ds(r0, CHUNK)
        ap, cv = cref[0, own], cref[1, own]
        lam, mu2 = cref[3, own], cref[4, own]
        vt, vp, vr = (ref[c, pl.ds(r0 + 2, CHUNK)] for c in range(3))
        e_tt = at * diff_t(ref, 0, r0, CHUNK) + ir * vr
        e_pp = ap * diff_p(vp) + cv * vt + ir * vr
        e_rr = diff_r(vr)
        e_tp = at * diff_t(ref, 1, r0, CHUNK) - cv * vp + ap * diff_p(vt)
        e_tr = diff_r(vt) - ir * vt + at * diff_t(ref, 2, r0, CHUNK)
        e_pr = diff_r(vp) - ir * vp + ap * diff_p(vr)
        dil = lam * (e_tt + e_pp + e_rr)
        shear = 0.5 * mu2
        return (dil + mu2 * e_tt, shear * e_tr, shear * e_tp, dil + mu2 * e_pp, shear * e_pr, dil + mu2 * e_rr)

    def local_velocity(step, f):
        ref = stress.at[step, f]

        def body(i, carry):
            r0 = i * CHUNK
            own = pl.ds(r0, CHUNK)
            forces = force_terms(ref, range(6), coef, r0)
            scale = coef[2, own]
            for c, force in enumerate(forces):
                value = scale * force
                if step > 0:
                    value = value + vel[step - 1, f, c, pl.ds(r0 + 2, CHUNK)]
                if f == 0:
                    if c == 2:
                        value = value + source[step, own]
                else:
                    value = value + inject[step, c, own]
                part_v[f, c, own] = value
            return carry

        lax.fori_loop(0, ROWS // CHUNK, body, 0)

        if step == 0:
            for c in range(3):
                values = [
                    part_v[f, c, row] + state_in[f, pl.ds(c * (LEV * ROWS) + row, LEV, stride=ROWS), :]
                    for row in range(ROWS)
                ]
                for row in range(ROWS):
                    part_v[f, c, row] = values[row]
        packed = pack_rim(blank, INNER, lambda c, row: part_v[f, c, row])
        for group in range(2):
            part_rim[f, group] = packed[group]

    def send_finished(phase, f, kind, rims, ref, lon_row):
        base = [part_rim[f, group] + coef_rim[kind, group] * rims[group] for group in range(2)]
        packed = pack_rim(base, BOUNDARY, lon_row)
        for group in range(2):
            lon_send[phase + 1, f, group] = packed[group]
        copies = send_cols(phase + 1, f, ref)
        send_lons(phase + 1, f)
        return copies

    def finish_velocity(step, f, rows, rims, bands=None):
        band_of = (TT, TP, TR)
        done = {}
        for row in rows:
            for c in range(3):
                extra = coef[0, row] * rim_of(rims, c, row)
                if bands is not None:
                    extra = extra + at * bands[band_of[c], row]
                done[c, row] = part_v[f, c, row] + coef[2, row] * extra
        for (c, row), value in done.items():
            vel[step, f, c, 2 + row] = value
        return done

    def edges_velocity(step, f):
        phase = 2 * step
        wait_halo(phase, f)
        rims = rim_terms(phase, f)
        done = finish_velocity(step, f, BOUNDARY, rims, band_terms(phase, f, (1, -1, 1)))
        copies = send_finished(phase, f, 0, rims, vel.at[step, f], lambda c, row: done[c, row])
        return rims, copies

    def local_stress(step, f):
        ref = vel.at[step, f]
        old = stress.at[step, f]

        def body(i, carry):
            r0 = i * CHUNK
            own = pl.ds(r0, CHUNK)
            for c, rate in enumerate(stress_terms(ref, coef, r0)):
                part_s[f, c, own] = old[c, pl.ds(r0 + 2, CHUNK)] + rate
            return carry

        lax.fori_loop(0, ROWS // CHUNK, body, 0)
        if step < STEPS - 1:
            packed = pack_rim(blank, INNER, lambda c, row: part_s[f, TP + c, row])
            for group in range(2):
                part_rim[f, group] = packed[group]

    def finish_stress(step, f, rows, rims, bands=None):
        last = step == STEPS - 1
        done = {}

        def put(c, row, value):
            done[c, row] = value

        for row in rows:
            ap, lam, mu2 = coef[0, row], coef[3, row], coef[4, row]
            half = 0.5 * mu2
            d_p = [ap * rim_of(rims, c, row) for c in range(3)]
            if bands is not None:
                d_t = [at * bands[c, row] for c in range(3)]
                dil = lam * (d_t[0] + d_p[1])
                put(TT, row, part_s[f, TT, row] + (dil + mu2 * d_t[0]))
                put(TP, row, part_s[f, TP, row] + half * (d_t[1] + d_p[0]))
                put(TR, row, part_s[f, TR, row] + half * d_t[2])
            else:
                dil = lam * d_p[1]
                put(TT, row, part_s[f, TT, row] + dil)
                put(TP, row, part_s[f, TP, row] + half * d_p[0])
                put(TR, row, part_s[f, TR, row])
            put(PP, row, part_s[f, PP, row] + (dil + mu2 * d_p[1]))
            put(RR, row, part_s[f, RR, row] + dil)
            put(PR, row, part_s[f, PR, row] + half * d_p[2])
        if last:
            finals = {(c, row): zone_or(STATE_OF[c], f, row, value) for (c, row), value in done.items()}
            for (c, row), value in finals.items():
                state_o[f, pl.ds(STATE_OF[c] * (LEV * ROWS) + row, LEV, stride=ROWS), :] = value
        else:
            for (c, row), value in done.items():
                stress[step + 1, f, c, 2 + row] = value
        return done

    def edges_stress(step, f):
        phase = 2 * step + 1
        wait_halo(phase, f)
        rims = rim_terms(phase, f)
        done = finish_stress(step, f, BOUNDARY, rims, band_terms(phase, f, (-1, -1, 1)))
        copies = []
        if step < STEPS - 1:
            copies = send_finished(phase, f, 1, rims, stress.at[step + 1, f], lambda c, row: done[TP + c, row])
        return rims, copies

    def materials():
        def body(i, carry):
            own = pl.ds(i * CHUNK, CHUNK)
            ids = jnp.stack([ids_in[pl.ds(i * CHUNK + k, LEV, stride=ROWS), :] for k in range(CHUNK)])
            rho = jnp.zeros((CHUNK, LEV, LANES), F32)
            lam, mu = rho, rho
            for layer in range(16):
                hit = ids == layer
                rho = jnp.where(hit, density_ref[layer], rho)
                lam = jnp.where(hit, lame_ref[layer], lam)
                mu = jnp.where(hit, shear_ref[layer], mu)
            coef[2, own] = step_size * (1.0 / rho)
            coef[3, own] = step_size * lam
            coef[4, own] = (2.0 * step_size) * mu
            return carry

        lax.fori_loop(0, ROWS // CHUNK, body, 0)
        packed = (
            pack_rim(blank, INNER, lambda c, row: coef[2, row] * coef[0, row]),
            pack_rim(
                blank,
                INNER,
                lambda c, row: coef[0, row] * (coef[3, row] + coef[4, row] if c == 1 else 0.5 * coef[4, row]),
            ),
        )
        for kind in range(2):
            for group in range(2):
                coef_rim[kind, group] = packed[kind][group]

    def spread(values, place_hit, lane_hot):
        high = values.astype(jnp.bfloat16).astype(F32)
        rest = values - high
        middle = rest.astype(jnp.bfloat16).astype(F32)
        total = None
        for term in (high, middle, rest - middle):
            left_hot = jnp.where(place_hit, term, 0.0).astype(jnp.bfloat16)
            piece = lax.dot_general(left_hot, lane_hot, (((1,), (1,)), ((), ())), preferred_element_type=F32)
            total = piece if total is None else total + piece
        return total.reshape(ROWS, LEV, LANES)

    def injection():
        plane = lat_cells * lon_cells
        rows = lax.broadcasted_iota(jnp.int32, (ROWS, LEV, LANES), 0) + lat * ROWS
        levels = lax.broadcasted_iota(jnp.int32, (ROWS, LEV, LANES), 1)
        lanes = lax.broadcasted_iota(jnp.int32, (ROWS, LEV, LANES), 2) + lon * LANES
        cell = levels * plane + rows * lon_cells + lanes
        adds = [jnp.zeros((ROWS, LEV, LANES), F32) for _ in range(STEPS)]
        for s in range(src_ref.shape[0]):
            hit = cell == src_ref[s]
            for step in range(STEPS):
                adds[step] = adds[step] + jnp.where(hit, wave_ref[step, s], 0.0)
        for step in range(STEPS):
            source[step] = adds[step]
        cells = cells_ref[...].reshape(1, -1)
        count = cells.shape[1]
        lev_n = lax.div(cells, plane)
        in_plane = cells - lev_n * plane
        row_n = lax.div(in_plane, lon_cells)
        col_n = in_plane - row_n * lon_cells - lon * LANES
        row_n = row_n - lat * ROWS
        inside = (row_n >= 0) & (row_n < ROWS)
        place_n = jnp.where(inside, row_n * LEV + lev_n, -1)
        index = lax.broadcasted_iota(jnp.int32, (LANES, count), 0)
        lane_hot = jnp.where(index == col_n, 1.0, 0.0).astype(jnp.bfloat16)
        place_hit = index == place_n

        def body(c, carry):
            for step in range(STEPS):
                inject[step, c] = spread(resid_ref[c, pl.ds(step, 1)], place_hit, lane_hot)
            return carry

        lax.fori_loop(0, 3, body, 0)

    ZROWS = 2 * ROWS
    side = lax.rem(lane, 64)
    own_at = 16 * is_e
    strip_at = 8 + 8 * is_e
    own_side = (side >= own_at) & (side < own_at + 16)
    own_slot = lax.div(lax.rem(lane - own_at + 64, 64), 16)
    strip_slot = lax.div(lax.rem(lane - strip_at + 64, 64), 8)

    def pack_channel(ch, rows_of):
        strips = [jnp.zeros((LEV, LANES), F32)] * 2
        owns = [[jnp.zeros((LEV, LANES), F32)] * 2 for _ in range(2)]
        window = []
        for row in range(ROWS):
            h, q = divmod(row, 8)
            fwd, adj = rows_of(row)
            both = jnp.where(lane < 64, lane_roll(fwd, 16), lane_roll(adj, 80))
            window.append(both)
            moved = lane_roll(both, 8 * q) if q else both
            strips[h] = jnp.where(strip_slot == q, moved, strips[h])
            moved = lane_roll(both, 16 * (q % 4)) if q % 4 else both
            owns[h][q // 4] = jnp.where(own_slot == q % 4, moved, owns[h][q // 4])
        for row in range(ROWS):
            zone[ch, 2 + 8 + row] = window[row]
        for h in range(2):
            strip_pack[h, ch] = strips[h]
            for g in range(2):
                own_pack[h, ch, g] = owns[h][g]

    def zone_pack_strips():
        def body(ch, carry):
            def rows_of(row):
                rows = pl.ds(ch * (LEV * ROWS) + row, LEV, stride=ROWS)
                return state_in[0, rows, :], state_in[1, rows, :]

            pack_channel(ch, rows_of)
            return carry

        lax.fori_loop(0, 9, body, 0)
        pack_channel(9, lambda row: (ids_in[pl.ds(row, LEV, stride=ROWS), :].astype(F32),) * 2)

    def zone_copy(kind):
        src, dst, slot, peer = (
            (own_pack.at[0], own_recv.at[1 - is_top], 1 - is_top, up),
            (own_pack.at[1], own_recv.at[is_bot], is_bot, down),
            (strip_pack, strip_mid, 2, across),
            (strip_pack.at[0], strip_recv.at[1 - is_top], 4 - is_top, across_up),
            (strip_pack.at[1], strip_recv.at[is_bot], 3 + is_bot, across_down),
        )[kind]
        return pltpu.make_async_remote_copy(
            src_ref=src,
            dst_ref=dst,
            send_sem=zone_ssem.at[kind],
            recv_sem=zone_rsem.at[slot],
            device_id=peer,
            device_id_type=MESH,
        )

    def zone_wait(slot):
        ref = (own_recv.at[0], own_recv.at[1], strip_mid, strip_recv.at[0], strip_recv.at[1])[slot]
        pltpu.make_async_remote_copy(
            src_ref=ref,
            dst_ref=ref,
            send_sem=zone_ssem.at[slot],
            recv_sem=zone_rsem.at[slot],
            device_id=up,
            device_id_type=MESH,
        ).wait_recv()

    def zone_start():
        zone_pack_strips()

        @pl.when(is_w == 1)
        def _():
            for kind in (2, 3, 4):
                zone_copy(kind).start()

    def zone_start_own():
        zone_copy(0).start()
        zone_copy(1).start()

    def zone_receive():
        for slot in (2, 3, 4):
            zone_wait(slot)

        @pl.when(is_e == 1)
        def _():
            for kind in (2, 3, 4):
                zone_copy(kind).start()

        for slot in (0, 1):
            zone_wait(slot)
        flips = (1.0 - 2.0 * is_top.astype(F32), 1.0 - 2.0 * is_bot.astype(F32))

        def body(ch, carry):
            middle = []
            for row in range(ROWS):
                h, q = divmod(row, 8)
                strip = lane_roll(strip_mid[h, ch], -8 * q) if q else strip_mid[h, ch]
                middle.append(jnp.where(own_side, zone[ch, 2 + 8 + row], strip))
            for row in range(ROWS):
                zone[ch, 2 + 8 + row] = middle[row]
            turns = (ch < 2) | (ch == 7) | (ch == 8)
            for slot, pole, first in ((0, is_top, 0), (1, is_bot, 24)):
                flip = jnp.where(turns, flips[slot], 1.0)
                values = []
                for q in range(8):
                    own = own_recv[slot, ch, q // 4]
                    own = lane_roll(own, -16 * (q % 4)) if q % 4 else own
                    strip = strip_recv[slot, ch]
                    strip = lane_roll(strip, -8 * q) if q else strip
                    values.append(jnp.where(own_side, own, strip) * flip)
                for q in range(8):
                    zone[ch, 2 + first + q] = jnp.where(pole == 1, values[7 - q], values[q])
            return carry

        lax.fori_loop(0, 10, body, 0)

    def zone_wait_sends():
        for kind in range(5):
            zone_copy(kind).wait_send()

    def zone_cells():
        row = lax.broadcasted_iota(jnp.int32, (ZROWS, LEV, LANES), 0) + (lat * ROWS - 8)
        col = lax.broadcasted_iota(jnp.int32, (ZROWS, LEV, LANES), 2) + (lon * LANES + 112 - 128 * is_e + lon_cells)
        turned = (row < 0) | (row >= lat_cells)
        row = jnp.where(row < 0, -1 - row, jnp.where(row >= lat_cells, 2 * lat_cells - 1 - row, row))
        col = lax.rem(col + jnp.where(turned, lon_cells // 2, 0), lon_cells)
        return row, col

    def zone_metrics():
        row = lax.broadcasted_iota(jnp.int32, (ZROWS, LEV, LANES), 0) + (lat * ROWS - 8)
        beyond = (row < 0) | (row >= lat_cells)
        row = jnp.where(row < 0, -1 - row, jnp.where(row >= lat_cells, 2 * lat_cells - 1 - row, row))
        theta = (row.astype(F32) + 0.5) * theta_step
        sines = jnp.maximum(jnp.sin(theta), SIN_FLOOR) * jnp.where(beyond, -1.0, 1.0)
        zcoef[0] = ir[None] / (sines * (12.0 * phi_step))
        zcoef[1] = jnp.cos(theta) / sines * ir[None]

    def zone_materials():
        def body(i, carry):
            row = pl.ds(2 + i * CHUNK, CHUNK)
            ids = zone[9, pl.ds(4 + i * CHUNK, CHUNK)].astype(jnp.int32)
            rho = jnp.ones((CHUNK, LEV, LANES), F32)
            lam, mu = rho, rho
            for layer in range(16):
                hit = ids == layer
                rho = jnp.where(hit, density_ref[layer], rho)
                lam = jnp.where(hit, lame_ref[layer], lam)
                mu = jnp.where(hit, shear_ref[layer], mu)
            zcoef[2, row] = step_size * (1.0 / rho)
            zcoef[3, row] = step_size * lam
            zcoef[4, row] = (2.0 * step_size) * mu
            return carry

        lax.fori_loop(0, (ZROWS - 4) // CHUNK, body, 0)

    def zone_injection():
        plane = lat_cells * lon_cells
        row, col = zone_cells()
        level3 = lax.broadcasted_iota(jnp.int32, (ZROWS, LEV, LANES), 1)
        lane3 = lax.broadcasted_iota(jnp.int32, (ZROWS, LEV, LANES), 2)
        cell = jnp.where(lane3 < 32, level3 * plane + row * lon_cells + col, -1)
        cells = cells_ref[...].reshape(1, -1)
        count = cells.shape[1]
        lev_n = lax.div(cells, plane)
        in_plane = cells - lev_n * plane
        row_n = lax.div(in_plane, lon_cells)
        first = lon * LANES + 112 - 128 * is_e
        col_n = lax.rem(in_plane - row_n * lon_cells - first + 2 * lon_cells, lon_cells)
        over_n = lax.rem(col_n + lon_cells // 2, lon_cells)
        straight = row_n - (lat * ROWS - 8)
        turned = jnp.where(row_n < 8, 7 - row_n, lat_cells - 1 - row_n + 24)
        can_turn = ((row_n < 8) & (is_top == 1)) | ((row_n >= lat_cells - 8) & (is_bot == 1))
        is_turned = can_turn & (over_n < 32)
        is_straight = (straight >= 0) & (straight < ZROWS) & (col_n < 32)
        zrow_n = jnp.where(is_turned, turned, straight)
        zcol_n = jnp.where(is_turned, over_n, col_n) + 64
        place_n = jnp.where(is_turned | is_straight, zrow_n * LEV + lev_n, -1)
        sign_n = jnp.where(is_turned, -1.0, 1.0)
        index = lax.broadcasted_iota(jnp.int32, (LANES, count), 0)
        lane_hot = jnp.where(index == zcol_n, 1.0, 0.0).astype(jnp.bfloat16)
        for part in range(2):
            place_hit = index + part * LANES == place_n
            signs = sign_n

            def body(c, carry):
                for step in range(STEPS):
                    values = resid_ref[c, pl.ds(step, 1)] * jnp.where(c < 2, signs, 1.0)
                    zinject[step, c, part * ROWS : (part + 1) * ROWS] = spread(values, place_hit, lane_hot)
                return carry

            lax.fori_loop(0, 3, body, 0)
        adds = [jnp.zeros((ZROWS, LEV, LANES), F32) for _ in range(STEPS)]
        for s in range(src_ref.shape[0]):
            hit = cell == src_ref[s]
            for step in range(STEPS):
                adds[step] = adds[step] + jnp.where(hit, wave_ref[step, s], 0.0)
        for step in range(STEPS):
            zinject[step, 2] += adds[step]

    def zone_steps():
        for step in range(STEPS):

            def velocity_body(i, carry):
                r0 = 2 + 4 * step + i * CHUNK
                own = pl.ds(r0, CHUNK)
                scale = zcoef[2, own]
                for c, force in enumerate(force_terms(zone, STATE_OF, zcoef, r0)):
                    zone[c, pl.ds(r0 + 2, CHUNK)] += scale * force + zinject[step, c, own]
                return carry

            lax.fori_loop(0, 7 - 2 * step, velocity_body, 0)
            density = None
            for c in range(3):
                new = zone[c, 2 + 8 : 2 + 8 + ROWS]
                term = new * lane_roll(new, 64)
                density = term if density is None else density + term
            zdensity[...] = density if step == 0 else zdensity[...] + density

            def stress_body(i, carry):
                r0 = 4 + 4 * step + i * CHUNK
                for c, rate in enumerate(stress_terms(zone, zcoef, r0)):
                    zone[STATE_OF[c], pl.ds(r0 + 2, CHUNK)] += rate
                return carry

            lax.fori_loop(0, 6 - 2 * step, stress_body, 0)

    seam_side = (lane >= LANES * (1 - is_e) - 8 * is_w) & (lane < LANES - (LANES - 8) * is_e)

    def zone_or(ch, f, row, value):
        return jnp.where(seam_side, lane_roll(zone[ch, 2 + 8 + row], -16 - 64 * f), value)

    started = []
    for f in range(2):
        loads[f].wait()
        unpack_stress(f, range(3), BOUNDARY)
    pl.semaphore_wait(barrier, 4 - is_e + 2 * is_w)
    for f in range(2):
        started += send_cols(0, f, stress.at[0, f])
    for f in range(2):
        unpack_stress(f, range(3), INNER)
        unpack_stress(f, range(3, 6), range(ROWS))
        packed = pack_rim(blank, range(ROWS), lambda c, row: stress[0, f, TP + c, 2 + row])
        for group in range(2):
            lon_send[0, f, group] = packed[group]
        send_lons(0, f)
    for load in loads[2:]:
        load.wait()

    @pl.when(is_w == 1)
    def _():
        zone_start()

    materials()
    injection()
    for step in range(STEPS):
        for f in range(2):
            local_velocity(step, f)
        if step == 1:

            @pl.when(at_seam == 1)
            def _():
                zone_injection()

        rims = []
        for f in range(2):
            rim, copies = edges_velocity(step, f)
            rims.append(rim)
            started += copies
        for f in range(2):
            for rows in INNER_GROUPS:
                finish_velocity(step, f, rows, rims[f])
            local_stress(step, f)
        if step == 0:

            @pl.when(is_e == 1)
            def _():
                zone_start()

            @pl.when(at_seam == 1)
            def _():
                zone_start_own()
                zone_metrics()

        if step == STEPS - 1:

            @pl.when(at_seam == 1)
            def _():
                zone_receive()
                zone_materials()
                zone_steps()

            densities = []
            for row in range(ROWS):
                density = None
                for s in range(STEPS):
                    for c in range(3):
                        term = vel[s, 0, c, 2 + row] * vel[s, 1, c, 2 + row]
                        density = term if density is None else density + term
                densities.append(jnp.where(seam_side, lane_roll(zdensity[row], -16), density))
            for row in range(ROWS):
                kern_o[pl.ds(row, LEV, stride=ROWS), :] = densities[row]
            for f in range(2):
                for c in range(3):
                    values = [zone_or(c, f, row, vel[step, f, c, 2 + row]) for row in range(ROWS)]
                    for row in range(ROWS):
                        state_o[f, pl.ds(c * (LEV * ROWS) + row, LEV, stride=ROWS), :] = values[row]
        rims = []
        for f in range(2):
            rim, copies = edges_stress(step, f)
            rims.append(rim)
            started += copies
        for f in range(2):
            for rows in INNER_GROUPS:
                finish_stress(step, f, rows, rims[f])

    for copy in started:
        copy.wait_send()
    for phase in range(2 * STEPS):
        for f in range(2):
            for slot, seam in ((0, is_w), (1, is_e)):

                @pl.when(seam == 0)
                def _():
                    lon_copy(phase, f, slot).wait_send()

    @pl.when(at_seam == 1)
    def _():
        zone_wait_sends()


def store(state_ref, kern_ref, fwd_out, adj_out, kern_out, sem):
    copies = [
        pltpu.make_async_copy(state_ref.at[0], fwd_out, sem.at[0]),
        pltpu.make_async_copy(state_ref.at[1], adj_out, sem.at[1]),
        pltpu.make_async_copy(kern_ref, kern_out, sem.at[2]),
    ]
    for copy in copies:
        copy.start()
    for copy in copies:
        copy.wait()


def on_device(n_lon, n_lat, forward, adjoint, layer_ids, density, lame, shear, src, wave, cells, resid):
    flat = 9 * LEV * ROWS
    vmem = pl.BlockSpec(memory_space=pltpu.VMEM)
    smem = pl.BlockSpec(memory_space=pltpu.SMEM)
    hbm = pl.BlockSpec(memory_space=pl.ANY)
    phases = 2 * STEPS
    state, kern = pl.pallas_call(
        functools.partial(kernel, n_lon, n_lat),
        out_shape=(pltpu.VMEM((2, flat, LANES), F32), pltpu.VMEM((LEV * ROWS, LANES), F32)),
        in_specs=[hbm, hbm, hbm, smem, smem, smem, smem, smem, vmem, vmem],
        out_specs=(vmem, vmem),
        scratch_shapes=[
            pltpu.VMEM((2, flat, LANES), F32),
            pltpu.VMEM((LEV * ROWS, LANES), jnp.int32),
            pltpu.VMEM((STEPS, 2, 6, ROWS + 4, LEV, LANES), F32),
            pltpu.VMEM((STEPS, 2, 3, ROWS + 4, LEV, LANES), F32),
            pltpu.VMEM((2, 3, ROWS, LEV, LANES), F32),
            pltpu.VMEM((2, 6, ROWS, LEV, LANES), F32),
            pltpu.VMEM((STEPS, 3, ROWS, LEV, LANES), F32),
            pltpu.VMEM((STEPS, ROWS, LEV, LANES), F32),
            pltpu.VMEM((5, ROWS, LEV, LANES), F32),
            pltpu.VMEM((2, 2, LEV, LANES), F32),
            pltpu.VMEM((2, 2, LEV, LANES), F32),
            pltpu.VMEM((phases, 2, 2, 3, 2, LEV, LANES), F32),
            pltpu.VMEM((phases, 2, 2, LEV, LANES), F32),
            pltpu.VMEM((phases, 2, 2, 2, LEV, LANES), F32),
            pltpu.VMEM((10, 2 * ROWS + 4, LEV, LANES), F32),
            pltpu.VMEM((5, 2 * ROWS, LEV, LANES), F32),
            pltpu.VMEM((STEPS, 3, 2 * ROWS, LEV, LANES), F32),
            pltpu.VMEM((ROWS, LEV, LANES), F32),
            pltpu.VMEM((2, 10, 2, LEV, LANES), F32),
            pltpu.VMEM((2, 10, 2, LEV, LANES), F32),
            pltpu.VMEM((2, 10, LEV, LANES), F32),
            pltpu.VMEM((2, 10, LEV, LANES), F32),
            pltpu.VMEM((2, 10, LEV, LANES), F32),
            pltpu.SemaphoreType.DMA((5,)),
            pltpu.SemaphoreType.DMA((phases, 2, 2)),
            pltpu.SemaphoreType.DMA((phases, 2, 2)),
            pltpu.SemaphoreType.DMA((phases, 2, 2)),
            pltpu.SemaphoreType.DMA((phases, 2, 2)),
            pltpu.SemaphoreType.DMA((5,)),
            pltpu.SemaphoreType.DMA((5,)),
        ],
        compiler_params=pltpu.CompilerParams(collective_id=0, has_side_effects=True),
        name="elastic_steps",
    )(
        forward.reshape(flat, LANES),
        adjoint.reshape(flat, LANES),
        layer_ids.reshape(LEV * ROWS, LANES),
        density,
        lame,
        shear,
        src,
        wave,
        cells,
        jnp.transpose(resid, (1, 0, 2)),
    )
    fwd, adj, kern = pl.pallas_call(
        store,
        out_shape=(
            jax.ShapeDtypeStruct((flat, LANES), F32),
            jax.ShapeDtypeStruct((flat, LANES), F32),
            jax.ShapeDtypeStruct((LEV * ROWS, LANES), F32),
        ),
        in_specs=[vmem, vmem],
        out_specs=(hbm, hbm, hbm),
        scratch_shapes=[pltpu.SemaphoreType.DMA((3,))],
        compiler_params=pltpu.CompilerParams(vmem_limit_bytes=1 << 20),
        name="store",
    )(pltpu.with_memory_space_constraint(state, pltpu.VMEM), pltpu.with_memory_space_constraint(kern, pltpu.VMEM))
    return fwd.reshape(forward.shape), adj.reshape(adjoint.shape), kern.reshape(layer_ids.shape)


def solution(mesh):
    field = P(None, None, "colat", "lon")
    plane = P(None, "colat", "lon")
    return jax.shard_map(
        functools.partial(on_device, mesh.shape["lon"], mesh.shape["colat"]),
        mesh=mesh,
        in_specs=(field, field, plane) + (P(),) * 7,
        out_specs=(field, field, plane),
        check_vma=False,
    )
```
